256 devices in a mesh: kv: 8 (over x, core), seq: 8 (over z), vocab: 4 (over y).
Axes of the slice: x: 4, y: 4, z: 8, core: 2. Of those that a mesh axis runs over, the one named last changes fastest.
Arguments:
- hidden_state: bfloat16 [48, 4, 3584], P('kv', 'vocab', 'seq'), may hold values from -6 to 6
- input_projection: bfloat16 [3584, 8, 1024], P('seq', 'kv'), may hold values from -0.09375 to 0.09375
- output_projection: bfloat16 [8, 512, 3584], P('kv', None, 'seq'), may hold values from -0.09375 to 0.09375
- norm_pre_attention: float32 [3584], P('seq'), may hold values from 0.1 to 1.9
- norm_post_attention: float32 [3584], P('seq'), may hold values from 0.1 to 1.9
- norm_pre_feedforward: float32 [3584], P('seq'), may hold values from 0.1 to 1.9
- norm_post_feedforward: float32 [3584], P('seq'), may hold values from 0.1 to 1.9
- norm_final: float32 [3584], P('seq'), may hold values from 0.1 to 1.9
- cache_keys: bfloat16 [4, 16384, 8, 256], P('vocab', 'seq', 'kv')
- cache_values: bfloat16 [4, 16384, 8, 256], P('vocab', 'seq', 'kv')
- cache_length: int32 [4], P('vocab'), may hold values from 1 to 16379, as said below
- ancestors: int32 [4, 48, 48], P('vocab'), may hold values from 0 to 1, as said below
- accepted_path: int32 [4, 5], P('vocab'), may hold values from 0 to 47, as said below
- gate_up_weight: bfloat16 [3584, 2, 14336], P('seq', None, ('kv', 'vocab')), may hold values from -0.09375 to 0.09375
- down_weight: bfloat16 [14336, 3584], P(('kv', 'vocab'), 'seq'), may hold values from -0.046875 to 0.046875
- draft_weight: bfloat16 [4, 3584, 3584], P(None, 'seq', ('kv', 'vocab')), may hold values from -0.09375 to 0.09375
- draft_bias: float32 [4, 3584], P(None, ('kv', 'vocab')), may hold values from -3 to 3
- vocab_weight: bfloat16 [131072, 3584], P(('kv', 'seq', 'vocab'))
- candidate_tokens: int32 [5, 48, 4, 8], replicated, may hold values from 0 to 131071
Outputs:
- keys_updated: bfloat16 [4, 16384, 8, 256], P('vocab', 'seq', 'kv')
- values_updated: bfloat16 [4, 16384, 8, 256], P('vocab', 'seq', 'kv')
- log_normalizer: float32 [5, 48, 4], replicated
- candidate_logits: float32 [5, 48, 4, 8], replicated
The draws below stay inside these ranges and needn't reach their ends.
Inputs may be any that keep to these rules, and one draw needn't show every extreme that they name: The first cache_length[k] slots of tenant k's cache are filled; in every draw some tenant holds exactly 16379. ancestors[k, t, u] is 1 exactly when u is t or an ancestor of t in tenant k's tree; node 0 is the root and every parent has a lower index than its child. accepted_path[k] lists 5 nodes of tenant k's tree from the root down, each the parent of the next; the last of them is node 47.
All inputs are finite; a program needn't handle non-finite values.
Results may differ from the reference program's by a relative error of at most 0.02.
Values may be sent and summed in bfloat16 or wider, within the bound.
A program may use at most 64 MiB of HBM per device.

```python
import math
import jax
import jax.numpy as jnp
from jax import lax

MODEL_WIDTH = 3584
QUERY_HEADS = 16
KEY_VALUE_HEADS = 8
HEAD_SIZE = 256
FF = 14336
NDRAFT = 4
TREE_NODES = 48
ACCEPT = 5
CAND = 8
NHEAD = 5
TENANT_COUNT = 4
CACHE_SLOTS = 16384
V = 131072


def cache_field(key, salt):
    field_key = jax.random.fold_in(key, salt)
    noise_key, scale_random_key = jax.random.split(field_key, 2)
    array_shape = (TENANT_COUNT, CACHE_SLOTS, KEY_VALUE_HEADS, HEAD_SIZE)
    row_norm_scale = jnp.exp(jax.random.uniform(scale_random_key, (TENANT_COUNT, CACHE_SLOTS, KEY_VALUE_HEADS, 1), minval=-0.8, maxval=0.8))
    values = jax.random.normal(noise_key, array_shape) * row_norm_scale
    return jnp.clip(values, -8.0, 8.0).astype(jnp.bfloat16)


def draw_cache_keys(key, part):
    return cache_field(key, 101)


def draw_cache_values(key, part):
    return cache_field(key, 202)


def draw_vocab_weight(key, part):
    noise_key, scale_random_key = jax.random.split(jax.random.fold_in(key, 303), 2)
    row_norm_scale = 10.0 ** jax.random.uniform(scale_random_key, (V,))
    noise_part = jax.random.normal(noise_key, (V, MODEL_WIDTH))
    return (jnp.clip(noise_part * row_norm_scale[:, None], -30.0, 30.0) / math.sqrt(MODEL_WIDTH)).astype(jnp.bfloat16)


def draw_cache_length(key, part):
    first_key, second_key = jax.random.split(jax.random.fold_in(key, 404))
    lengths = jax.random.randint(first_key, (TENANT_COUNT,), 1, CACHE_SLOTS - ACCEPT + 1)
    longest = jax.random.randint(second_key, (), 0, TENANT_COUNT)
    return jnp.where(jnp.arange(TENANT_COUNT) == longest, CACHE_SLOTS - ACCEPT, lengths).astype(jnp.int32)


def tree_draw(key):
    backsteps = jax.random.randint(jax.random.fold_in(key, 505), (TENANT_COUNT, TREE_NODES), 0, 3)
    tree_nodes = jnp.arange(TREE_NODES, dtype=jnp.int32)
    parents = jnp.maximum(tree_nodes - 1 - jnp.minimum(backsteps, jnp.maximum(tree_nodes - 1, 0)), 0).astype(jnp.int32)
    parents = jnp.where(tree_nodes[None, :] <= ACCEPT - 2, jnp.maximum(tree_nodes - 1, 0)[None, :], parents).astype(jnp.int32)
    identity = (tree_nodes[:, None] == tree_nodes[None, :]).astype(jnp.int32)

    def build_tree(parent_row):

        def extend(node_index, ancestry):
            parent_line = lax.dynamic_index_in_dim(ancestry, parent_row[node_index], 0, True)
            self_line = lax.dynamic_index_in_dim(identity, node_index, 0, True)
            return lax.dynamic_update_slice(ancestry, jnp.maximum(parent_line, self_line), (node_index, jnp.int32(0)))
        ancestry = lax.fori_loop(1, TREE_NODES - 1, extend, identity)
        node_depth = jnp.sum(ancestry, axis=-1) - 1
        eligible = (node_depth == ACCEPT - 2) & (tree_nodes < TREE_NODES - 1)
        last_parent = jnp.max(jnp.where(eligible, tree_nodes, 0)).astype(jnp.int32)
        parent_line = lax.dynamic_index_in_dim(ancestry, last_parent, 0, True)
        self_line = identity[TREE_NODES - 1:TREE_NODES]
        return lax.dynamic_update_slice(ancestry, jnp.maximum(parent_line, self_line), (jnp.int32(TREE_NODES - 1), jnp.int32(0)))
    ancestry = jax.vmap(build_tree)(parents)
    deepest = ancestry[:, TREE_NODES - 1, :]
    ranking = jnp.argsort((1 - deepest) * TREE_NODES + tree_nodes[None, :], axis=-1, stable=True)
    return (ancestry.astype(jnp.int32), ranking[:, :ACCEPT].astype(jnp.int32))


def draw_ancestors(key, part):
    return tree_draw(key)[0]


def draw_accepted_path(key, part):
    return tree_draw(key)[1]


def plant(result, stream_key, smallest, largest):
    spot = [jax.random.randint(jax.random.fold_in(stream_key, axis), (), 0, length) for axis, length in enumerate(result.shape)]
    widest = result.shape.index(max(result.shape))
    neighbour = spot[:widest] + [(spot[widest] + 1) % result.shape[widest]] + spot[widest + 1:]
    return result.at[tuple(spot)].set(smallest).at[tuple(neighbour)].set(largest)


def steps_of(key, shape, cuts, low, high):
    loudness, own = 1.0, jax.random.fold_in(key, 6)
    for position, shards_of in cuts:
        heights = jnp.exp(jax.random.uniform(jax.random.fold_in(own, position), (shards_of,), jnp.float32, low / len(cuts), high / len(cuts)))
        loudness = loudness * jnp.repeat(heights, shape[position] // shards_of).reshape([-1 if axis == position else 1 for axis in range(len(shape))])
    return loudness


def scatter_about(key, dims, width, bound, cuts=(), kind=jnp.bfloat16):
    result = width * jax.random.normal(key, dims, jnp.float32)
    if cuts:
        result = result * steps_of(key, dims, cuts, -0.22, 0.18)
    return jnp.clip(result, -bound, bound).astype(kind)


def setup_inputs(seed: int = 0) -> dict:
    key_list = jax.random.split(jax.random.key(seed), 20)
    hidden_state = scatter_about(key_list[0], (TREE_NODES, TENANT_COUNT, MODEL_WIDTH), 1.0, 6.0, ((0, 8), (1, 4), (2, 8)))
    input_projection = scatter_about(key_list[1], (MODEL_WIDTH, KEY_VALUE_HEADS, 4 * HEAD_SIZE), MODEL_WIDTH ** -0.5, 0.09375, ((0, 8), (1, 8)))
    output_projection = scatter_about(key_list[2], (KEY_VALUE_HEADS, 2 * HEAD_SIZE, MODEL_WIDTH), (QUERY_HEADS * HEAD_SIZE) ** -0.5, 0.09375, ((0, 8), (2, 8)))
    norm_pre_attention = jnp.clip(1.0 + 0.18 * jax.random.normal(key_list[3], (MODEL_WIDTH,), jnp.float32), 0.1, 1.9)
    norm_post_attention = jnp.clip(1.0 + 0.18 * jax.random.normal(key_list[4], (MODEL_WIDTH,), jnp.float32), 0.1, 1.9)
    norm_pre_feedforward = jnp.clip(1.0 + 0.18 * jax.random.normal(key_list[5], (MODEL_WIDTH,), jnp.float32), 0.1, 1.9)
    norm_post_feedforward = jnp.clip(1.0 + 0.18 * jax.random.normal(key_list[6], (MODEL_WIDTH,), jnp.float32), 0.1, 1.9)
    norm_final = jnp.clip(1.0 + 0.18 * jax.random.normal(key_list[7], (MODEL_WIDTH,), jnp.float32), 0.1, 1.9)
    cache_keys = draw_cache_keys(jax.random.fold_in(key_list[19], 71), 0)
    cache_values = draw_cache_values(jax.random.fold_in(key_list[19], 71), 0)
    cache_length = draw_cache_length(jax.random.fold_in(key_list[19], 71), 0)
    ancestors = draw_ancestors(jax.random.fold_in(key_list[19], 71), 0)
    accepted_path = draw_accepted_path(jax.random.fold_in(key_list[19], 71), 0)
    gate_up_weight = scatter_about(key_list[13], (MODEL_WIDTH, 2, FF), MODEL_WIDTH ** -0.5, 0.09375, ((0, 8), (2, 32)))
    down_weight = scatter_about(key_list[14], (FF, MODEL_WIDTH), FF ** -0.5, 0.046875, ((0, 32), (1, 8)))
    draft_weight = scatter_about(key_list[15], (NDRAFT, MODEL_WIDTH, MODEL_WIDTH), MODEL_WIDTH ** -0.5, 0.09375, ((1, 8), (2, 32)))
    draft_bias = scatter_about(key_list[16], (NDRAFT, MODEL_WIDTH), 0.5, 3.0, ((1, 32),), jnp.float32)
    vocab_weight = draw_vocab_weight(jax.random.fold_in(key_list[19], 71), 0)
    candidate_tokens = plant(jax.random.randint(key_list[18], (NHEAD, TREE_NODES, TENANT_COUNT, CAND), 0, V), jax.random.fold_in(key_list[18], 1), 0, V - 1).astype(jnp.int32)
    return dict(hidden_state=hidden_state, input_projection=input_projection, output_projection=output_projection, norm_pre_attention=norm_pre_attention, norm_post_attention=norm_post_attention, norm_pre_feedforward=norm_pre_feedforward, norm_post_feedforward=norm_post_feedforward, norm_final=norm_final, cache_keys=cache_keys, cache_values=cache_values, cache_length=cache_length, ancestors=ancestors, accepted_path=accepted_path, gate_up_weight=gate_up_weight, down_weight=down_weight, draft_weight=draft_weight, draft_bias=draft_bias, vocab_weight=vocab_weight, candidate_tokens=candidate_tokens)


EPSILON = 1e-06
SCORE_CAP = 50.0
LOGIT_CAP = 30.0

def inverse_square_root(values):
    return lax.rsqrt(lax.optimization_barrier(jnp.mean(values * values, axis=-1, keepdims=True)) + EPSILON)

def apply_rotary(vectors, token_positions):
    half_dim = vectors.shape[-1] // 2
    frequency = 10000.0 ** (-2.0 * jnp.arange(half_dim, dtype=jnp.float32) / vectors.shape[-1])
    angles = token_positions.astype(jnp.float32)[..., None] * frequency
    cosine = jnp.cos(angles)
    sine_part = jnp.sin(angles)
    first_half = vectors[..., :half_dim]
    second_half = vectors[..., half_dim:]
    return jnp.concatenate([first_half * cosine - second_half * sine_part, second_half * cosine + first_half * sine_part], axis=-1)

def capped_weight(scores):
    return jnp.exp(SCORE_CAP * jnp.tanh(scores * 0.0625 / SCORE_CAP))

def attend_tenant(query_rows, keys_all, values_all, new_keys, new_values, length, ancestry):
    query_float = query_rows.astype(jnp.float32)
    scores = jnp.einsum('thgc,shc->thgs', query_float, keys_all.astype(jnp.float32))
    filled = jnp.arange(keys_all.shape[0], dtype=jnp.int32) < length
    weights = jnp.where(filled[None, None, None, :], capped_weight(scores), 0.0)
    tree_scores = jnp.einsum('thgc,uhc->thgu', query_float, new_keys.astype(jnp.float32))
    tree_weights = jnp.where(ancestry[:, None, None, :] > 0, capped_weight(tree_scores), 0.0)
    denominator = lax.optimization_barrier(jnp.sum(weights, axis=-1)) + lax.optimization_barrier(jnp.sum(tree_weights, axis=-1))
    rounded = lax.optimization_barrier(weights.astype(jnp.bfloat16)).astype(jnp.float32)
    tree_rounded = lax.optimization_barrier(tree_weights.astype(jnp.bfloat16)).astype(jnp.float32)
    numerator = jnp.einsum('thgs,shc->thgc', rounded, values_all.astype(jnp.float32))
    numerator = numerator + jnp.einsum('thgu,uhc->thgc', tree_rounded, new_values.astype(jnp.float32))
    return (numerator / denominator[..., None]).astype(jnp.bfloat16)

def reference(hidden_state, input_projection, output_projection, norm_pre_attention, norm_post_attention, norm_pre_feedforward, norm_post_feedforward, norm_final, cache_keys, cache_values, cache_length, ancestors, accepted_path, gate_up_weight, down_weight, draft_weight, draft_bias, vocab_weight, candidate_tokens):
    all_rows = TREE_NODES * TENANT_COUNT
    residual_stream = hidden_state.astype(jnp.float32)
    depths = lax.optimization_barrier(jnp.sum(ancestors, axis=-1)).astype(jnp.int32) - 1
    token_positions = jnp.transpose(cache_length[:, None] + depths)
    scaled_input = (residual_stream * norm_pre_attention).astype(jnp.bfloat16).reshape(all_rows, MODEL_WIDTH)
    projected_rows = jnp.dot(scaled_input, input_projection.reshape(MODEL_WIDTH, KEY_VALUE_HEADS * 4 * HEAD_SIZE), preferred_element_type=jnp.float32)
    projected_rows = projected_rows.reshape(TREE_NODES, TENANT_COUNT, KEY_VALUE_HEADS, 4 * HEAD_SIZE) * inverse_square_root(residual_stream)[..., None]
    query_rows = apply_rotary(projected_rows[..., :2 * HEAD_SIZE].reshape(TREE_NODES, TENANT_COUNT, KEY_VALUE_HEADS, 2, HEAD_SIZE), token_positions[:, :, None, None]).astype(jnp.bfloat16)
    new_keys = apply_rotary(projected_rows[..., 2 * HEAD_SIZE:3 * HEAD_SIZE], token_positions[:, :, None]).astype(jnp.bfloat16)
    new_values = projected_rows[..., 3 * HEAD_SIZE:].astype(jnp.bfloat16)
    outputs = []
    for tenant in range(TENANT_COUNT):
        outputs.append(attend_tenant(query_rows[:, tenant], cache_keys[tenant], cache_values[tenant], new_keys[:, tenant], new_values[:, tenant], cache_length[tenant], ancestors[tenant]))
    attended = jnp.stack(outputs, axis=1).reshape(all_rows, QUERY_HEADS * HEAD_SIZE)
    attention_out = jnp.dot(attended, output_projection.reshape(QUERY_HEADS * HEAD_SIZE, MODEL_WIDTH), preferred_element_type=jnp.float32)
    flat_residual = residual_stream.reshape(all_rows, MODEL_WIDTH)
    first_sum = (flat_residual + attention_out * inverse_square_root(attention_out) * norm_post_attention).astype(jnp.bfloat16)
    first_float = first_sum.astype(jnp.float32)
    scaled_ffn = (first_float * norm_pre_feedforward).astype(jnp.bfloat16)
    gate_up = jnp.dot(scaled_ffn, gate_up_weight.reshape(MODEL_WIDTH, 2 * FF), preferred_element_type=jnp.float32) * inverse_square_root(first_float)
    activated = (jax.nn.gelu(gate_up[:, :FF], approximate=True) * gate_up[:, FF:]).astype(jnp.bfloat16)
    ffn_out = jnp.dot(activated, down_weight, preferred_element_type=jnp.float32)
    second_sum = (first_float + ffn_out * inverse_square_root(ffn_out) * norm_post_feedforward).astype(jnp.bfloat16)
    second_float = second_sum.astype(jnp.float32)
    normed = (second_float * inverse_square_root(second_float) * norm_final).astype(jnp.bfloat16)
    branches = []
    for draft_index in range(NDRAFT):
        lifted = jnp.dot(normed, draft_weight[draft_index], preferred_element_type=jnp.float32) + draft_bias[draft_index]
        branches.append(jax.nn.silu(lifted).astype(jnp.bfloat16))
    branch = jnp.stack(branches, axis=0).reshape(NDRAFT * all_rows, MODEL_WIDTH)
    candidates = candidate_tokens.reshape(NHEAD, all_rows, CAND)
    piece_count = 64
    piece_rows = V // piece_count
    stacked = vocab_weight.reshape(piece_count, piece_rows, MODEL_WIDTH)
    offsets = jnp.arange(piece_count, dtype=jnp.int32) * piece_rows

    def scan_piece(running, inputs):
        totals, picked = running
        matrix, offset = inputs
        base_logits = lax.dot_general(normed, matrix, (((1,), (1,)), ((), ())), preferred_element_type=jnp.float32)
        draft_extra = lax.dot_general(branch, matrix, (((1,), (1,)), ((), ())), preferred_element_type=jnp.float32)
        draft_extra = draft_extra.reshape(NDRAFT, all_rows, piece_rows)
        raw_logits = jnp.concatenate([base_logits[None], base_logits[None] + draft_extra], axis=0)
        logits = LOGIT_CAP * jnp.tanh(raw_logits / LOGIT_CAP)
        totals = totals + lax.optimization_barrier(jnp.sum(jnp.exp(logits), axis=-1))
        columns = offset + jnp.arange(piece_rows, dtype=jnp.int32)
        matches = candidates[..., None] == columns
        picked = picked + lax.optimization_barrier(jnp.sum(jnp.where(matches, logits[:, :, None, :], 0.0), axis=-1))
        return ((totals, picked), None)
    start_state = (jnp.zeros((NHEAD, all_rows), jnp.float32), jnp.zeros((NHEAD, all_rows, CAND), jnp.float32))
    (totals, picked), _ = lax.scan(scan_piece, start_state, (stacked, offsets))
    log_normalizer = jnp.log(totals).reshape(NHEAD, TREE_NODES, TENANT_COUNT)
    candidate_logits = picked.reshape(NHEAD, TREE_NODES, TENANT_COUNT, CAND)
    tenant_index = jnp.arange(TENANT_COUNT, dtype=jnp.int32)[:, None]
    keys_tenant = jnp.transpose(new_keys, (1, 0, 2, 3))
    values_tenant = jnp.transpose(new_values, (1, 0, 2, 3))
    chosen_keys = keys_tenant[tenant_index, accepted_path]
    chosen_values = values_tenant[tenant_index, accepted_path]
    slot_rows = cache_length[:, None] + jnp.arange(ACCEPT, dtype=jnp.int32)
    keys_updated = cache_keys.at[tenant_index, slot_rows].set(chosen_keys)
    values_updated = cache_values.at[tenant_index, slot_rows].set(chosen_values)
    return (keys_updated, values_updated, log_normalizer, candidate_logits)
```

```python
import jax
import jax.numpy as jnp
import numpy as np
from jax import lax
from jax.experimental import pallas as pl
from jax.experimental.pallas import tpu as pltpu
from jax.sharding import PartitionSpec as P

MESH = pl.DeviceIdType.MESH
F32 = jnp.float32
BF16 = jnp.bfloat16
WIDTH = 3584
EPSILON = 1e-06
SCORE_CAP = 50.0
LOGIT_CAP = 30.0
NT = (((1,), (1,)), ((), ()))


def rem(a, n):
    return lax.rem(a, jnp.int32(n))


def div(a, n):
    return lax.div(a, jnp.int32(n))


def dot(a, b):
    return jnp.dot(a, b, preferred_element_type=F32)


def dot_nt(a, b):
    return lax.dot_general(a, b, NT, preferred_element_type=F32)


def iota(shape, dim):
    return lax.broadcasted_iota(jnp.int32, shape, dim)


def send(src, dst, ssem, rsem, peer):
    pltpu.make_async_remote_copy(
        src_ref=src,
        dst_ref=dst,
        send_sem=ssem,
        recv_sem=rsem,
        device_id=peer,
        device_id_type=MESH,
    ).start()


def wait_bytes(ref, sem):
    pltpu.make_async_copy(ref, ref, sem).wait()


def plane_peer(p, d):
    q = rem(p + d, 32)
    return q, {"kv": div(q, 4), "vocab": rem(q, 4)}


def position_in_mesh():
    return lax.axis_index("kv"), lax.axis_index("seq"), lax.axis_index("vocab")


def project_kernel(
    h_ref, w_hbm, g_ref, anc_ref, len_ref, freq_ref, p48_ref,
    q_ref, k_ref, v_ref,
    w, pad8, xg, xf, ps, prc, sqs, sqr, agc, wsem, ssem, rsem,
):
    kv, z, _ = position_in_mesh()
    load = pltpu.make_async_copy(w_hbm, w, wsem)
    load.start()
    barrier = pltpu.get_barrier_semaphore()
    for d in range(1, 8):
        pl.semaphore_signal(barrier, inc=1, device_id={"kv": rem(kv + d, 8)}, device_id_type=MESH)
        pl.semaphore_signal(barrier, inc=1, device_id={"seq": rem(z + d, 8)}, device_id_type=MESH)
    pad8[...] = jnp.zeros_like(pad8)
    pad8[0:6, :] = h_ref[...].astype(F32)
    xg[kv] = pad8[...].astype(BF16)
    pl.semaphore_wait(barrier, 14)
    for d in range(1, 8):
        send(xg.at[kv], xg.at[kv], ssem.at[0], rsem.at[0], {"kv": rem(kv + d, 8)})
    depth = jnp.sum(anc_ref[...].astype(F32), axis=1, keepdims=True) - 1.0
    angle = (len_ref[0].astype(F32) + depth) * freq_ref[...]
    cosine = jnp.cos(angle)
    sine = jnp.sin(angle)
    load.wait()
    wait_bytes(xg.at[0:7], rsem.at[0])
    for j in range(8):
        xf[8 * j : 8 * j + 8, :] = xg[j].astype(F32)
    x = dot(p48_ref[...], xf[...].astype(BF16))
    eye = iota((48, 128), 0) == iota((48, 128), 1)
    squares = jnp.sum(x * x, axis=1, keepdims=True)
    row = jnp.sum(jnp.where(eye, squares, 0.0), axis=0, keepdims=True)
    sqs[...] = jnp.broadcast_to(row, (8, 128))
    part = dot((x * g_ref[...]).astype(BF16), w[...])
    for j in range(8):
        ps[j] = part[:, 128 * j : 128 * j + 128].astype(BF16)
    for d in range(1, 8):
        other = rem(z + d, 8)
        send(ps.at[other], prc.at[d - 1], ssem.at[1], rsem.at[1], {"seq": other})
        send(sqs, sqr.at[d - 1], ssem.at[2], rsem.at[2], {"seq": other})
    wait_bytes(sqr, rsem.at[2])
    total = sqs[...]
    for j in range(7):
        total = total + sqr[j]
    column = jnp.sum(jnp.where(eye, total[0:1, :], 0.0), axis=1, keepdims=True)
    inverse = lax.rsqrt(column / WIDTH + EPSILON)
    wait_bytes(prc, rsem.at[1])
    chunk = ps[z].astype(F32)
    for j in range(7):
        chunk = chunk + prc[j].astype(F32)
    agc[z] = (chunk * inverse).astype(BF16)
    for d in range(1, 8):
        send(agc.at[z], agc.at[z], ssem.at[3], rsem.at[3], {"seq": rem(z + d, 8)})
    wait_bytes(agc.at[0:7], rsem.at[3])
    for j, (ref, row0) in enumerate(((q_ref, 0), (q_ref, 48), (k_ref, 0))):
        first = agc[2 * j].astype(F32)
        second = agc[2 * j + 1].astype(F32)
        ref[row0 : row0 + 48, 0:128] = (first * cosine - second * sine).astype(BF16)
        ref[row0 : row0 + 48, 128:256] = (second * cosine + first * sine).astype(BF16)
    v_ref[:, 0:128] = agc[6]
    v_ref[:, 128:256] = agc[7]
    wait_bytes(xg.at[0:7], ssem.at[0])
    wait_bytes(prc, ssem.at[1])
    wait_bytes(sqr, ssem.at[2])
    wait_bytes(agc.at[0:7], ssem.at[3])


def capped_weight(scores):
    return jnp.exp(SCORE_CAP * jnp.tanh(scores * (0.0625 / SCORE_CAP)))


def attend_kernel(
    len_ref, path_ref, q_ref, kn_ref, vn_ref, anc_ref, keys_ref, values_ref,
    keys_out, values_out, num_out, den_out,
    num, den,
):
    step = pl.program_id(0)
    rows = keys_ref.shape[0]
    z = lax.axis_index("seq")
    length = len_ref[0]
    start = z * (rows * pl.num_programs(0)) + step * rows

    @pl.when(step == 0)
    def _():
        num[...] = jnp.zeros_like(num)
        den[...] = jnp.zeros_like(den)

    keys = keys_ref[...]
    values = values_ref[...]
    keys_out[...] = keys
    values_out[...] = values

    @pl.when((start + rows > length) & (start < length + 5))
    def _():
        away = start + iota((rows, 1), 0) - length
        target = jnp.full((rows, 1), -1, jnp.int32)
        for a in range(5):
            target = jnp.where(away == a, path_ref[0, a], target)
        selector = jnp.where(iota((rows, 48), 1) == target, 1.0, 0.0).astype(BF16)
        inside = jnp.broadcast_to(target, (rows, 256)) >= 0
        for fresh, old, out in ((kn_ref, keys, keys_out), (vn_ref, values, values_out)):
            out[...] = jnp.where(inside, dot(selector, fresh[...]), old.astype(F32)).astype(BF16)

    @pl.when(start < length)
    def _():
        weights = capped_weight(dot_nt(q_ref[...], keys))
        filled = iota((96, rows), 1) < length - start
        weights = jnp.where(filled, weights, 0.0)
        den[...] += jnp.sum(weights, axis=1, keepdims=True)
        num[...] += dot(weights.astype(BF16), values)

    @pl.when(step == pl.num_programs(0) - 1)
    def _():
        anc = jnp.where(z == 0, anc_ref[...], 0)
        for g in range(2):
            block = slice(48 * g, 48 * g + 48)
            weights = capped_weight(dot_nt(q_ref[block, :], kn_ref[...]))
            weights = jnp.where(anc > 0, weights, 0.0)
            den[block, :] += jnp.sum(weights, axis=1, keepdims=True)
            num[block, :] += dot(weights.astype(BF16), vn_ref[...])
        for j in range(8):
            num_out[j] = num[
                24 * (j // 2) : 24 * (j // 2) + 24, 128 * (j % 2) : 128 * (j % 2) + 128
            ].astype(BF16)
        eye = iota((96, 128), 0) == iota((96, 128), 1)
        row = jnp.sum(jnp.where(eye, den[...], 0.0), axis=0, keepdims=True)
        den_out[...] = jnp.broadcast_to(row, (8, 128))


def moments(values):
    lane = iota((8, 128), 1)
    tile = jnp.zeros((8, 128), F32)
    for i, v in enumerate(values):
        tile = jnp.where(lane == i, jnp.sum(v, axis=1, keepdims=True), tile)
    return tile


def finish_kernel(
    num_ref, den_ref, h_ref, wo_ref, gpa_ref, gpf_ref, gqf_ref, gfin_ref,
    wgu_hbm, wdown_hbm, wdraft_hbm, bias_ref, vocab_hbm, cand_ref,
    e64_ref, p192_ref, e256_ref, p96_ref,
    logn_ref, pick_ref,
    wgu, wdown, wdraft, wv, wp,
    nr, dr, ga, af, os_, orr, pad8, ms, mr, fp, xf, gs, gr, ags, acts, ds, dsr, ms2, mr2,
    npl, nz, nzs, nbo, nb, lf, dsl, dslr, bias, zb, bf, bs, big, basef, bbase, base4, tokb, tokd,
    rz, rzr, rp, accb, accd,
    wsem, ssem, rsem,
):
    kv, z, y = position_in_mesh()
    core = rem(kv, 2)
    p = kv * 4 + y
    loads = [
        pltpu.make_async_copy(wgu_hbm, wgu, wsem.at[0]),
        pltpu.make_async_copy(wdown_hbm, wdown, wsem.at[1]),
        pltpu.make_async_copy(wdraft_hbm, wdraft, wsem.at[2]),
        pltpu.make_async_copy(vocab_hbm, wv, wsem.at[3]),
    ]
    for load in loads:
        load.start()
    barrier = pltpu.get_barrier_semaphore()
    for d in range(1, 8):
        pl.semaphore_signal(barrier, inc=1, device_id={"seq": rem(z + d, 8)}, device_id_type=MESH)

    @pl.loop(1, 32)
    def _(d):
        pl.semaphore_signal(barrier, inc=1, device_id=plane_peer(p, d)[1], device_id_type=MESH)

    pl.semaphore_wait(barrier, 38)

    def to_seq(src, dst, s):
        for d in range(1, 8):
            other = rem(z + d, 8)
            send(src(other), dst(d), ssem.at[s], rsem.at[s], {"seq": other})

    def to_plane(src, dst, s):
        @pl.loop(1, 32)
        def _(d):
            q, peer = plane_peer(p, d)
            send(src(q), dst(d), ssem.at[s], rsem.at[s], peer)

    to_seq(lambda o: num_ref.at[o], lambda d: nr.at[d - 1], 0)
    to_seq(lambda o: den_ref, lambda d: dr.at[d - 1], 1)
    pad8[...] = jnp.zeros_like(pad8)
    pad8[0:6, :] = h_ref[...].astype(F32)
    wait_bytes(dr, rsem.at[1])
    total = den_ref[...]
    for j in range(7):
        total = total + dr[j]
    pick_lane = iota((24, 128), 1) == iota((24, 128), 0) + 24 * div(z, 2)
    den = jnp.sum(jnp.where(pick_lane, total[0:1, :], 0.0), axis=1, keepdims=True)
    wait_bytes(nr, rsem.at[0])
    num = num_ref[z].astype(F32)
    for j in range(7):
        num = num + nr[j].astype(F32)
    ga[z] = (num / den).astype(BF16)
    to_seq(lambda o: ga.at[z], lambda d: ga.at[z], 2)
    wait_bytes(ga.at[0:7], rsem.at[2])
    for j in range(8):
        r0, c0 = 24 * ((j // 2) % 2), 256 * (j // 4) + 128 * (j % 2)
        af[r0 : r0 + 24, c0 : c0 + 128] = ga[j].astype(F32)
    attended = dot(e64_ref[...], af[...].astype(BF16)).astype(BF16)
    out = dot_nt(attended, wo_ref[...])
    for j in range(8):
        os_[j] = out[8 * j : 8 * j + 8, :].astype(BF16)
    for d in range(1, 8):
        other = rem(kv + d, 8)
        send(os_.at[other], orr.at[d - 1], ssem.at[3], rsem.at[3], {"kv": other})
    hidden = pad8[...]
    wait_bytes(orr, rsem.at[3])
    att = os_[kv].astype(F32)
    for j in range(7):
        att = att + orr[j].astype(F32)
    gained = att * gpa_ref[...]
    ms[...] = moments((att * att, hidden * gained, gained * gained, hidden * hidden))
    to_seq(lambda o: ms, lambda d: mr.at[d - 1], 4)
    wait_bytes(mr, rsem.at[4])
    tot = ms[...]
    for j in range(7):
        tot = tot + mr[j]
    inv = lax.rsqrt(tot[:, 0:1] / WIDTH + EPSILON)
    first = (hidden + gained * inv).astype(BF16).astype(F32)
    square = tot[:, 3:4] + 2.0 * inv * tot[:, 1:2] + inv * inv * tot[:, 2:3]
    inv = lax.rsqrt(jnp.maximum(square, 0.0) / WIDTH + EPSILON)
    fp[p] = (first * inv * gpf_ref[...]).astype(BF16)
    to_plane(lambda q: fp.at[p], lambda d: fp.at[p], 5)
    loads[0].wait()
    wait_bytes(fp.at[0:31], rsem.at[5])
    for j in range(32):
        xf[8 * j : 8 * j + 8, :] = fp[j].astype(F32)
    x = dot(p192_ref[...], xf[...].astype(BF16)).astype(BF16)
    gu = dot(x, wgu[...])
    for j in range(8):
        gs[j] = gu[24 * j : 24 * j + 24, :].astype(BF16)
    to_seq(lambda o: gs.at[o], lambda d: gr.at[d - 1], 6)
    loads[1].wait()
    wait_bytes(gr, rsem.at[6])
    gu = gs[z].astype(F32)
    for j in range(7):
        gu = gu + gr[j].astype(F32)
    gate, up = gu[:, 0:448], gu[:, 448:896]
    gelu = 0.5 * gate * (1.0 + jnp.tanh(0.7978845608028654 * (gate + 0.044715 * gate * gate * gate)))
    ags[z] = (gelu * up).astype(BF16)
    to_seq(lambda o: ags.at[z], lambda d: ags.at[z], 7)
    wait_bytes(ags.at[0:7], rsem.at[7])
    for j in range(8):
        acts[24 * j : 24 * j + 24, :] = ags[j].astype(F32)
    act = dot(e256_ref[...], acts[...].astype(BF16)).astype(BF16)
    out = dot(act, wdown[...])
    for j in range(32):
        ds[j] = out[8 * j : 8 * j + 8, :].astype(BF16)
    to_plane(lambda q: ds.at[q], lambda d: dsr.at[d - 1], 8)
    loads[2].wait()
    loads[3].wait()
    spread = iota((896, 1024), 0) == (lax.shift_right_logical(iota((896, 1024), 1), 7) * 112 + (iota((896, 1024), 1) & 127))
    spread = jnp.where(spread & ((iota((896, 1024), 1) & 127) < 112), 1.0, 0.0).astype(BF16)
    for j in range(4):
        wp[0:512, 1024 * j : 1024 * j + 1024] = dot(
            wv[:, 896 * j : 896 * j + 896], spread
        ).astype(BF16)
    send(wp.at[0:512], wp.at[512:1024], ssem.at[9], rsem.at[9], {"kv": kv + 1 - 2 * core})
    wait_bytes(dsr, rsem.at[8])
    out = ds[p].astype(F32)
    for j in range(31):
        out = out + dsr[j].astype(F32)
    gained = out * gqf_ref[...]
    ms2[...] = moments((out * out, first * gained, gained * gained, first * first))
    to_seq(lambda o: ms2, lambda d: mr2.at[d - 1], 10)
    lf[...] = jnp.zeros_like(lf)
    bias[...] = jnp.zeros_like(bias)
    bias[0:4, 0:112] = bias_ref[...]
    wait_bytes(mr2, rsem.at[10])
    tot = ms2[...]
    for j in range(7):
        tot = tot + mr2[j]
    inv = lax.rsqrt(tot[:, 0:1] / WIDTH + EPSILON)
    second = (first + gained * inv).astype(BF16).astype(F32)
    square = tot[:, 3:4] + 2.0 * inv * tot[:, 1:2] + inv * inv * tot[:, 2:3]
    inv = lax.rsqrt(jnp.maximum(square, 0.0) / WIDTH + EPSILON)
    normed = (second * inv * gfin_ref[...]).astype(BF16)
    npl[p] = normed
    to_plane(lambda q: npl.at[p], lambda d: npl.at[p], 11)
    nz[z] = dot(normed, spread[0:448, 0:512]).astype(BF16)
    to_seq(lambda o: nz.at[z], lambda d: nz.at[z], 12)
    wait_bytes(npl.at[0:31], rsem.at[11])
    for j in range(32):
        xf[8 * j : 8 * j + 8, :] = npl[j].astype(F32)
    x = dot(p192_ref[...], xf[...].astype(BF16)).astype(BF16)
    for i in range(4):
        lf[i, :, 0:112] = dot(x, wdraft[i])
    for j in range(8):
        for i in range(4):
            dsl[j, i] = lf[i, 24 * j : 24 * j + 24, :].astype(BF16)
    to_seq(lambda o: dsl.at[o], lambda d: dslr.at[d - 1], 13)
    wait_bytes(nz.at[0:7], rsem.at[12])
    for j in range(8):
        nzs[:, 512 * j : 512 * j + 512] = nz[j].astype(F32)
    half = div(y, 2)
    slot = kv * 2 + rem(y, 2)
    nbo[...] = nzs[...].astype(BF16)

    @pl.loop(0, 16)
    def _(d):
        q = rem(div(kv, 2) * 4 + y + d, 16)
        target = 2 * div(q, 4) + half
        to_me = (d == 0) & (half == core)

        @pl.when(jnp.logical_not(to_me))
        def _():
            send(nbo, nb.at[slot], ssem.at[14], rsem.at[14], {"kv": target, "vocab": rem(q, 4)})

        @pl.when(to_me)
        def _():
            pltpu.make_async_copy(nbo, nb.at[slot], rsem.at[14]).start()

    wait_bytes(dslr, rsem.at[13])
    for i in range(4):
        lifted = dsl[z, i].astype(F32)
        for j in range(7):
            lifted = lifted + dslr[j, i].astype(F32)
        lifted = lifted + bias[i : i + 1, :]
        zb[z, i] = (lifted / (1.0 + jnp.exp(-lifted))).astype(BF16)
    to_seq(lambda o: zb.at[z], lambda d: zb.at[z], 15)
    wait_bytes(zb.at[0:7], rsem.at[15])
    for j in range(8):
        for i in range(4):
            bf[i, 24 * j : 24 * j + 24, :] = zb[j, i].astype(F32)
    for i in range(4):
        for hf in range(2):
            bs[hf, i] = bf[i, 96 * hf : 96 * hf + 96, :].astype(BF16)
    columns = pl.ds(pl.multiple_of(p * 128, 128), 128)

    @pl.loop(1, 32)
    def _(d):
        q, peer = plane_peer(p, d)
        send(bs.at[rem(div(q, 4), 2)], big.at[:, :, columns], ssem.at[16], rsem.at[16], peer)

    for i in range(4):
        big[i, :, columns] = bs[core, i]
    for n in range(5):
        for k in range(2):
            tokens = cand_ref[n, 2 * core + k]
            if n == 0:
                tokb[:, 48 * k : 48 * k + 48] = tokens
            else:
                lane = 96 * (n - 1) + 48 * k
                tokd[:, lane : lane + 48] = tokens
    linear = (kv * 8 + z) * 4 + y
    sibling = ((kv + 1 - 2 * core) * 8 + z) * 4 + y
    accb[...] = jnp.zeros_like(accb)
    accd[...] = jnp.zeros_like(accd)

    def score(raw, tokens, acc, lanes, first_id):
        logits = LOGIT_CAP * jnp.tanh(raw * (1.0 / LOGIT_CAP))
        where = iota(raw.shape, 0)
        local = tokens - first_id
        for c in range(8):
            hit = where == local[c : c + 1, :]
            acc[c : c + 1, 0:lanes] += jnp.sum(jnp.where(hit, logits, 0.0), axis=0, keepdims=True)
        acc[8:9, 0:lanes] += jnp.sum(jnp.exp(logits), axis=0, keepdims=True)

    def first_id(i):
        return jnp.where(i < 2, linear * 512 + 256 * i, sibling * 512 + 256 * (i - 2))

    wait_bytes(nb, rsem.at[14])
    for t in range(16):
        basef[8 * t : 8 * t + 8, :] = nb[t].astype(F32)
    bbase[...] = dot(p96_ref[...], basef[...].astype(BF16)).astype(BF16)
    wait_bytes(wp.at[0:512], rsem.at[9])

    @pl.loop(0, 4)
    def _(i):
        rows = pl.ds(pl.multiple_of(i * 256, 256), 256)
        raw = dot_nt(wp[rows, :], bbase[...])
        for d in range(4):
            base4[rows, 96 * d : 96 * d + 96] = raw
        score(raw, tokb[:, 0:96], accb, 96, first_id(i))

    wait_bytes(big.at[:, :, 0:3968], rsem.at[16])

    @pl.loop(0, 4)
    def _(i):
        rows = pl.ds(pl.multiple_of(i * 256, 256), 256)
        raw = dot_nt(wp[rows, :], big[...].reshape(384, 4096)) + base4[rows, :]
        score(raw, tokd[...], accd, 384, first_id(i))

    rz[:, 0:128] = accb[...].astype(BF16)
    rz[:, 128:512] = accd[...].astype(BF16)
    to_seq(lambda o: rz, lambda d: rzr.at[d - 1], 17)
    wait_bytes(rzr, rsem.at[17])
    res = rz[...].astype(F32)
    for j in range(7):
        res = res + rzr[j].astype(F32)
    rp[p] = res.astype(BF16)
    to_plane(lambda q: rp.at[p], lambda d: rp.at[p], 18)
    wait_bytes(rp.at[0:31], rsem.at[18])
    for c in range(2):
        res = jnp.zeros((16, 512), F32)
        for x4 in range(4):
            for yy in range(4):
                res = res + rp[(2 * x4 + c) * 4 + yy].astype(F32)
        logs = jnp.log(res[8:9, :])
        for n in range(5):
            for k in range(2):
                lane = 48 * k if n == 0 else 128 + 96 * (n - 1) + 48 * k
                logn_ref[n, 2 * c + k : 2 * c + k + 1, :] = logs[:, lane : lane + 48]
                pick_ref[n, 2 * c + k] = res[0:8, lane : lane + 48]

    for s, ref in (
        (0, nr), (1, dr), (2, ga.at[0:7]), (3, orr), (4, mr), (5, fp.at[0:31]), (6, gr),
        (7, ags.at[0:7]), (8, dsr), (9, wp.at[0:512]), (10, mr2), (11, npl.at[0:31]),
        (12, nz.at[0:7]), (13, dslr), (14, nb.at[0:15]), (15, zb.at[0:7]),
        (16, big.at[:, :, 0:3968]), (17, rzr), (18, rp.at[0:31]),
    ):
        wait_bytes(ref, ssem.at[s])

    @pl.when(half != core)
    def _():
        wait_bytes(nbo, ssem.at[14])


def one_hot_rows(rows, columns, places):
    table = np.zeros((rows, columns), np.float32)
    table[np.arange(rows), places] = 1.0
    return table


def tables():
    r48 = np.arange(48)
    p48 = one_hot_rows(48, 64, (r48 // 6) * 8 + r48 % 6)
    r192 = np.arange(192)
    tenant, node = r192 // 48, r192 % 48
    p192 = one_hot_rows(192, 256, ((node // 6) * 4 + tenant) * 8 + node % 6)
    r96 = np.arange(96)
    tenant, node = r96 // 48, r96 % 48
    p96 = one_hot_rows(96, 128, ((node // 6) * 2 + tenant) * 8 + node % 6)
    return p48, p192, p96


def vmem(shape, dtype=BF16):
    return pltpu.VMEM(shape, dtype)


VM = pl.BlockSpec(memory_space=pltpu.VMEM)
SM = pl.BlockSpec(memory_space=pltpu.SMEM)
ANY = pl.BlockSpec(memory_space=pl.ANY)
DMA = pltpu.SemaphoreType.DMA


def local(
    hidden_state,
    input_projection,
    output_projection,
    norm_pre_attention,
    norm_post_attention,
    norm_pre_feedforward,
    norm_post_feedforward,
    norm_final,
    cache_keys,
    cache_values,
    cache_length,
    ancestors,
    accepted_path,
    gate_up_weight,
    down_weight,
    draft_weight,
    draft_bias,
    vocab_weight,
    candidate_tokens,
):
    p48, p192, p96 = (jnp.asarray(t, BF16) for t in tables())
    e64, e256 = p48.T, p192.T
    frequency = 10000.0 ** (-2.0 * jnp.arange(128, dtype=F32) / 256)
    own = hidden_state.reshape(6, 448)
    anc = ancestors[0]
    queries, new_keys, new_values = pl.pallas_call(
        project_kernel,
        name="project",
        out_shape=(
            jax.ShapeDtypeStruct((96, 256), BF16),
            jax.ShapeDtypeStruct((48, 256), BF16),
            jax.ShapeDtypeStruct((48, 256), BF16),
        ),
        in_specs=[VM, ANY, VM, VM, SM, VM, VM],
        out_specs=(VM, VM, VM),
        scratch_shapes=[
            vmem((448, 1024)), vmem((8, 448), F32), vmem((8, 8, 448)), vmem((64, 448), F32),
            vmem((8, 48, 128)), vmem((7, 48, 128)), vmem((8, 128), F32), vmem((7, 8, 128), F32),
            vmem((8, 48, 128)), DMA, DMA((4,)), DMA((4,)),
        ],
        compiler_params=pltpu.CompilerParams(
            collective_id=0, has_side_effects=True, vmem_limit_bytes=32 << 20
        ),
    )(
        own, input_projection.reshape(448, 1024), norm_pre_attention.reshape(1, 448), anc,
        cache_length, frequency.reshape(1, 128), p48,
    )
    slots = cache_keys.shape[1]
    block = 512
    rowspec = pl.BlockSpec((block, 256), lambda i: (i, 0))

    def whole(shape):
        return pl.BlockSpec(shape, lambda i: (0,) * len(shape))

    keys_updated, values_updated, numerators, denominators = pl.pallas_call(
        attend_kernel,
        name="attend",
        grid=(slots // block,),
        out_shape=(
            jax.ShapeDtypeStruct((slots, 256), BF16),
            jax.ShapeDtypeStruct((slots, 256), BF16),
            jax.ShapeDtypeStruct((8, 24, 128), BF16),
            jax.ShapeDtypeStruct((8, 128), F32),
        ),
        in_specs=[
            SM, SM, whole((96, 256)), whole((48, 256)), whole((48, 256)), whole((48, 48)),
            rowspec, rowspec,
        ],
        out_specs=(rowspec, rowspec, whole((8, 24, 128)), whole((8, 128))),
        scratch_shapes=[vmem((96, 256), F32), vmem((96, 1), F32)],
        compiler_params=pltpu.CompilerParams(vmem_limit_bytes=32 << 20),
    )(
        cache_length, accepted_path, queries, new_keys, new_values, anc,
        cache_keys.reshape(slots, 256), cache_values.reshape(slots, 256),
    )
    log_normalizer, picked = pl.pallas_call(
        finish_kernel,
        name="finish",
        out_shape=(
            jax.ShapeDtypeStruct((5, 4, 48), F32),
            jax.ShapeDtypeStruct((5, 4, 8, 48), F32),
        ),
        in_specs=[VM] * 8 + [ANY] * 3 + [VM, ANY] + [VM] * 5,
        out_specs=(VM, VM),
        scratch_shapes=[
            vmem((448, 896)), vmem((448, 448)), vmem((4, 448, 112)), vmem((512, 3584)),
            vmem((1024, 4096)),
            vmem((7, 24, 128)), vmem((7, 8, 128), F32), vmem((8, 24, 128)), vmem((48, 512), F32),
            vmem((8, 8, 448)), vmem((7, 8, 448)), vmem((8, 448), F32),
            vmem((8, 128), F32), vmem((7, 8, 128), F32), vmem((32, 8, 448)), vmem((256, 448), F32),
            vmem((8, 24, 896)), vmem((7, 24, 896)), vmem((8, 24, 448)), vmem((192, 448), F32),
            vmem((32, 8, 448)), vmem((31, 8, 448)), vmem((8, 128), F32), vmem((7, 8, 128), F32),
            vmem((32, 8, 448)), vmem((8, 8, 512)), vmem((8, 4096), F32), vmem((8, 4096)),
            vmem((16, 8, 4096)),
            vmem((4, 192, 128), F32), vmem((8, 4, 24, 128)), vmem((7, 4, 24, 128)),
            vmem((8, 128), F32), vmem((8, 4, 24, 128)), vmem((4, 192, 128), F32),
            vmem((2, 4, 96, 128)), vmem((4, 96, 4096)), vmem((128, 4096), F32), vmem((96, 4096)),
            vmem((1024, 384), F32), vmem((8, 128), jnp.int32), vmem((8, 384), jnp.int32),
            vmem((16, 512)), vmem((7, 16, 512)), vmem((32, 16, 512)),
            vmem((16, 128), F32), vmem((16, 384), F32),
            DMA((4,)), DMA((19,)), DMA((19,)),
        ],
        compiler_params=pltpu.CompilerParams(
            collective_id=1, has_side_effects=True, vmem_limit_bytes=60 << 20
        ),
    )(
        numerators, denominators, own, output_projection[0].T,
        norm_post_attention.reshape(1, 448), norm_pre_feedforward.reshape(1, 448),
        norm_post_feedforward.reshape(1, 448), norm_final.reshape(1, 448),
        gate_up_weight.reshape(448, 896), down_weight, draft_weight, draft_bias, vocab_weight,
        jnp.transpose(candidate_tokens, (0, 2, 3, 1)), e64, p192, e256, p96,
    )
    return (
        keys_updated.reshape(cache_keys.shape),
        values_updated.reshape(cache_values.shape),
        jnp.transpose(log_normalizer, (0, 2, 1)),
        jnp.transpose(picked, (0, 3, 1, 2)),
    )


def solution(mesh):
    placed = (
        P("kv", "vocab", "seq"),
        P("seq", "kv", None),
        P("kv", None, "seq"),
        P("seq"),
        P("seq"),
        P("seq"),
        P("seq"),
        P("seq"),
        P("vocab", "seq", "kv", None),
        P("vocab", "seq", "kv", None),
        P("vocab"),
        P("vocab", None, None),
        P("vocab", None),
        P("seq", None, ("kv", "vocab")),
        P(("kv", "vocab"), "seq"),
        P(None, "seq", ("kv", "vocab")),
        P(None, ("kv", "vocab")),
        P(("kv", "seq", "vocab"), None),
        P(),
    )
    return jax.shard_map(
        local,
        mesh=mesh,
        in_specs=placed,
        out_specs=(P("vocab", "seq", "kv", None), P("vocab", "seq", "kv", None), P(), P()),
        check_vma=False,
    )
```

```python
import jax
import jax.numpy as jnp
import numpy as np
from jax import lax
from jax.experimental import pallas as pl
from jax.experimental.pallas import tpu as pltpu
from jax.sharding import PartitionSpec as P

MESH = pl.DeviceIdType.MESH
F32 = jnp.float32
BF16 = jnp.bfloat16
WIDTH = 3584
EPSILON = 1e-06
SCORE_CAP = 50.0
LOGIT_CAP = 30.0
NT = (((1,), (1,)), ((), ()))


def rem(a, n):
    return lax.rem(a, jnp.int32(n))


def div(a, n):
    return lax.div(a, jnp.int32(n))


def dot(a, b):
    return jnp.dot(a, b, preferred_element_type=F32)


def dot_nt(a, b):
    return lax.dot_general(a, b, NT, preferred_element_type=F32)


def iota(shape, dim):
    return lax.broadcasted_iota(jnp.int32, shape, dim)


def send(src, dst, ssem, rsem, peer):
    pltpu.make_async_remote_copy(
        src_ref=src,
        dst_ref=dst,
        send_sem=ssem,
        recv_sem=rsem,
        device_id=peer,
        device_id_type=MESH,
    ).start()


def wait_bytes(ref, sem):
    pltpu.make_async_copy(ref, ref, sem).wait()


def plane_peer(p, d):
    q = rem(p + d, 32)
    return q, {"kv": div(q, 4), "vocab": rem(q, 4)}


def position_in_mesh():
    return lax.axis_index("kv"), lax.axis_index("seq"), lax.axis_index("vocab")


def capped_weight(scores):
    return jnp.exp(SCORE_CAP * jnp.tanh(scores * (0.0625 / SCORE_CAP)))


def moments(values):
    lane = iota((8, 128), 1)
    tile = jnp.zeros((8, 128), F32)
    for i, v in enumerate(values):
        tile = jnp.where(lane == i, jnp.sum(v, axis=1, keepdims=True), tile)
    return tile


def rms_inverse(total):
    return lax.rsqrt(jnp.maximum(total, 0.0) / WIDTH + EPSILON)


LOADS = (
    "h", "p48", "g_att", "w_in", "freq", "anc", "keys", "values", "e64", "w_out", "g_post",
    "g_pre", "p192", "w_gu", "e256", "w_down", "g_fpost", "g_fin", "w_draft", "bias", "cand",
    "p96", "w_voc",
)


def step_kernel(len_ref, *refs):
    count = len(LOADS)
    source = dict(zip(LOADS, refs[:count]))
    kn, vn, res_ref = refs[count : count + 3]
    here = dict(zip(LOADS, refs[count + 3 : 2 * count + 3]))
    (
        wp, spread, pad8, xg, xf6, ps, prc, agc, qs,
        den, num, ns, nr, ga, af, os_, orr, ms, mr, fp, xf, gs, gr, ags, acts, ds, dsr,
        ms2, mr2, npl, nz, nzs, nbo, nb, lf, dsl, dslr, biasf, zbo, zb, bf, big, basef, bbase,
        base4, tokb, tokd, rz, rzr, rp, accb, accd,
        wsem, ssem, rsem, sring, r1, r2, r2h,
    ) = refs[2 * count + 3 :]
    kv, z, y = position_in_mesh()
    core = rem(kv, 2)
    x = div(kv, 2)
    p = kv * 4 + y
    sibling = kv + 1 - 2 * core
    copies = {}
    for i, name in enumerate(LOADS):
        copies[name] = pltpu.make_async_copy(source[name], here[name], wsem.at[i])
        copies[name].start()

    def get(name):
        copies[name].wait()
        return here[name]

    barrier = pltpu.get_barrier_semaphore()
    for d in range(1, 8):
        other = rem(z + d, 8)
        pl.semaphore_signal(barrier, inc=1, device_id={"seq": other}, device_id_type=MESH)
        pl.semaphore_signal(barrier, inc=1, device_id={"kv": sibling, "seq": other}, device_id_type=MESH)

    @pl.loop(1, 32)
    def _(d):
        pl.semaphore_signal(barrier, inc=1, device_id=plane_peer(p, d)[1], device_id_type=MESH)

    sent = []

    def to_seq(src, dst, s, total):
        for d in range(1, 8):
            other = rem(z + d, 8)
            send(src(other), dst(d), ssem.at[s], rsem.at[s], {"seq": other})
        sent.append((total, s))

    def to_kv(src, dst, s, total):
        for d in range(1, 8):
            other = rem(kv + d, 8)
            send(src(other), dst(d), ssem.at[s], rsem.at[s], {"kv": other})
        sent.append((total, s))

    def to_plane(src, dst, s, total):
        @pl.loop(1, 32)
        def _(d):
            q, peer = plane_peer(p, d)
            send(src(q), dst(d), ssem.at[s], rsem.at[s], peer)

        sent.append((total, s))

    pad8[...] = jnp.zeros_like(pad8)
    pad8[0:6, :] = get("h")[...].astype(F32)
    xg[kv] = pad8[...].astype(BF16)
    pl.semaphore_wait(barrier, 45)
    to_kv(lambda o: xg.at[kv], lambda d: xg.at[kv], 0, xg.at[0:7])
    depth = jnp.sum(get("anc")[...].astype(F32), axis=1, keepdims=True) - 1.0
    angle = (len_ref[0].astype(F32) + depth) * get("freq")[...]
    cosine = jnp.cos(angle)
    sine = jnp.sin(angle)
    eye = iota((96, 128), 0) == iota((96, 128), 1)
    p48 = get("p48")
    gain = get("g_att")[...]
    w_in = get("w_in")
    wait_bytes(xg.at[0:7], rsem.at[0])
    for j in range(8):
        xf6[8 * j : 8 * j + 8, :] = xg[j].astype(F32)
    tokens = dot(p48[...], xf6[...].astype(BF16))
    squares = jnp.sum(tokens * tokens, axis=1, keepdims=True)
    row = jnp.sum(jnp.where(eye[0:48], squares, 0.0), axis=0, keepdims=True)
    row = jnp.broadcast_to(row, (16, 128)).astype(BF16)
    part = dot((tokens * gain).astype(BF16), w_in[...])
    for j in range(8):
        ps[j, 0:48, :] = part[:, 128 * j : 128 * j + 128].astype(BF16)
        ps[j, 48:64, :] = row
    to_seq(lambda o: ps.at[o], lambda d: prc.at[d - 1], 1, prc)
    lane = iota((896, 1024), 1)
    inside = lane & 127
    place = lax.shift_right_logical(lane, 7) * 112 + inside
    spread[...] = jnp.where((iota((896, 1024), 0) == place) & (inside < 112), 1.0, 0.0).astype(BF16)
    wait_bytes(prc, rsem.at[1])
    chunk = ps[z].astype(F32)
    for j in range(7):
        chunk = chunk + prc[j].astype(F32)
    column = jnp.sum(jnp.where(eye[0:48], chunk[48:49, :], 0.0), axis=1, keepdims=True)
    agc[z] = (chunk[0:48] * rms_inverse(column)).astype(BF16)
    to_seq(lambda o: agc.at[z], lambda d: agc.at[z], 2, agc.at[0:7])
    keys, values = get("keys"), get("values")
    wait_bytes(agc.at[0:7], rsem.at[2])
    for j, (ref, row0) in enumerate(((qs, 0), (qs, 48), (kn, 0))):
        first = agc[2 * j].astype(F32)
        second = agc[2 * j + 1].astype(F32)
        ref[row0 : row0 + 48, 0:128] = (first * cosine - second * sine).astype(BF16)
        ref[row0 : row0 + 48, 128:256] = (second * cosine + first * sine).astype(BF16)
    vn[:, 0:128] = agc[6]
    vn[:, 128:256] = agc[7]

    queries = qs[...]
    anc = jnp.where(z == 0, here["anc"][...], 0)
    anc = jnp.concatenate([anc, anc], axis=0)
    weights = capped_weight(dot_nt(queries, kn[...]))
    weights = jnp.where(anc > 0, weights, 0.0)
    den[...] = jnp.sum(weights, axis=1, keepdims=True)
    num[...] = dot(weights.astype(BF16), vn[...])
    filled = len_ref[0] - z * 2048

    @pl.loop(0, 4)
    def _(i):
        rows = pl.ds(pl.multiple_of(i * 512, 512), 512)
        weights = capped_weight(dot_nt(queries, keys[rows, :]))
        weights = jnp.where(iota((96, 512), 1) < filled - i * 512, weights, 0.0)
        den[...] += jnp.sum(weights, axis=1, keepdims=True)
        num[...] += dot(weights.astype(BF16), values[rows, :])

    row = jnp.sum(jnp.where(eye, den[...], 0.0), axis=0, keepdims=True)
    row = jnp.broadcast_to(row, (16, 128)).astype(BF16)
    for j in range(8):
        r0, c0 = 24 * (j // 2), 128 * (j % 2)
        ns[j, 0:16, :] = row
        ns[j, 16:40, :] = num[r0 : r0 + 24, c0 : c0 + 128].astype(BF16)
    to_seq(lambda o: ns.at[o], lambda d: nr.at[d - 1], 3, nr)
    e64, w_out = get("e64"), get("w_out")
    wait_bytes(nr, rsem.at[3])
    total = ns[z].astype(F32)
    for j in range(7):
        total = total + nr[j].astype(F32)
    chosen = iota((24, 128), 1) == iota((24, 128), 0) + 24 * div(z, 2)
    below = jnp.sum(jnp.where(chosen, total[0:1, :], 0.0), axis=1, keepdims=True)
    ga[z] = (total[16:40, :] / below).astype(BF16)
    to_seq(lambda o: ga.at[z], lambda d: ga.at[z], 4, ga.at[0:7])
    w_voc = get("w_voc")

    def widen(j):
        wp[0:512, 1024 * j : 1024 * j + 1024] = dot(
            w_voc[:, 896 * j : 896 * j + 896], spread[...]
        ).astype(BF16)

    wait_bytes(ga.at[0:7], rsem.at[4])
    for j in range(8):
        r0, c0 = 24 * ((j // 2) % 2), 256 * (j // 4) + 128 * (j % 2)
        af[r0 : r0 + 24, c0 : c0 + 128] = ga[j].astype(F32)
    attended = dot(e64[...], af[...].astype(BF16)).astype(BF16)
    out = dot_nt(attended, w_out[...])
    for j in range(8):
        os_[j] = out[8 * j : 8 * j + 8, :].astype(BF16)
    to_kv(lambda o: os_.at[o], lambda d: orr.at[d - 1], 5, orr)
    hidden = pad8[...]
    gain = get("g_post")[...]
    wait_bytes(orr, rsem.at[5])
    att = os_[kv].astype(F32)
    for j in range(7):
        att = att + orr[j].astype(F32)
    gained = att * gain
    ms[...] = moments((att * att, hidden * gained, gained * gained, hidden * hidden))
    to_seq(lambda o: ms, lambda d: mr.at[d - 1], 6, mr)
    gain = get("g_pre")[...]
    wait_bytes(mr, rsem.at[6])
    tot = ms[...]
    for j in range(7):
        tot = tot + mr[j]
    inv = rms_inverse(tot[:, 0:1])
    first = (hidden + gained * inv).astype(BF16).astype(F32)
    inv = rms_inverse(tot[:, 3:4] + 2.0 * inv * tot[:, 1:2] + inv * inv * tot[:, 2:3])
    fp[p] = (first * inv * gain).astype(BF16)
    to_plane(lambda q: fp.at[p], lambda d: fp.at[p], 7, fp.at[0:31])
    widen(0)
    p192, w_gu = get("p192"), get("w_gu")
    wait_bytes(fp.at[0:31], rsem.at[7])
    for j in range(32):
        xf[8 * j : 8 * j + 8, :] = fp[j].astype(F32)
    rows192 = dot(p192[...], xf[...].astype(BF16)).astype(BF16)
    gu = dot(rows192, w_gu[...])
    for j in range(8):
        gs[j] = gu[24 * j : 24 * j + 24, :].astype(BF16)
    to_seq(lambda o: gs.at[o], lambda d: gr.at[d - 1], 8, gr)
    widen(1)
    widen(2)
    widen(3)
    send(wp.at[0:512], wp.at[512:1024], ssem.at[17], rsem.at[17], {"kv": sibling})
    sent.append((wp.at[0:512], 17))
    e256, w_down = get("e256"), get("w_down")
    wait_bytes(gr, rsem.at[8])
    gu = gs[z].astype(F32)
    for j in range(7):
        gu = gu + gr[j].astype(F32)
    gate, up = gu[:, 0:448], gu[:, 448:896]
    gelu = 0.5 * gate * (1.0 + jnp.tanh(0.7978845608028654 * (gate + 0.044715 * gate * gate * gate)))
    ags[z] = (gelu * up).astype(BF16)
    to_seq(lambda o: ags.at[z], lambda d: ags.at[z], 9, ags.at[0:7])
    cand = get("cand")
    for n in range(5):
        for k in range(2):
            ids = cand[n, 2 * core + k]
            if n == 0:
                tokb[:, 48 * k : 48 * k + 48] = ids
            else:
                at = 96 * (n - 1) + 48 * k
                tokd[:, at : at + 48] = ids
    lf[...] = jnp.zeros_like(lf)
    biasf[...] = jnp.zeros_like(biasf)
    biasf[0:4, 0:112] = get("bias")[...]
    accb[...] = jnp.zeros_like(accb)
    accd[...] = jnp.zeros_like(accd)
    wait_bytes(ags.at[0:7], rsem.at[9])
    for j in range(8):
        acts[24 * j : 24 * j + 24, :] = ags[j].astype(F32)
    act = dot(e256[...], acts[...].astype(BF16)).astype(BF16)
    out = dot(act, w_down[...])
    for j in range(32):
        ds[j] = out[8 * j : 8 * j + 8, :].astype(BF16)
    to_plane(lambda q: ds.at[q], lambda d: dsr.at[d - 1], 10, dsr)
    gain = get("g_fpost")[...]
    wait_bytes(dsr, rsem.at[10])
    out = ds[p].astype(F32)
    for j in range(31):
        out = out + dsr[j].astype(F32)
    gained = out * gain
    ms2[...] = moments((out * out, first * gained, gained * gained, first * first))
    to_seq(lambda o: ms2, lambda d: mr2.at[d - 1], 11, mr2)
    gain = get("g_fin")[...]
    w_draft = get("w_draft")
    wait_bytes(mr2, rsem.at[11])
    tot = ms2[...]
    for j in range(7):
        tot = tot + mr2[j]
    inv = rms_inverse(tot[:, 0:1])
    second = (first + gained * inv).astype(BF16).astype(F32)
    inv = rms_inverse(tot[:, 3:4] + 2.0 * inv * tot[:, 1:2] + inv * inv * tot[:, 2:3])
    normed = (second * inv * gain).astype(BF16)
    npl[p] = normed
    to_plane(lambda q: npl.at[p], lambda d: npl.at[p], 12, npl.at[0:31])
    nz[z] = dot(normed, spread[0:448, 0:512]).astype(BF16)
    to_seq(lambda o: nz.at[z], lambda d: nz.at[z], 13, nz.at[0:7])
    wait_bytes(npl.at[0:31], rsem.at[12])
    for j in range(32):
        xf[8 * j : 8 * j + 8, :] = npl[j].astype(F32)
    rows192 = dot(p192[...], xf[...].astype(BF16)).astype(BF16)
    for i in range(4):
        lf[i, :, 0:112] = dot(rows192, w_draft[i])
    for j in range(8):
        for i in range(4):
            dsl[j, i] = lf[i, 24 * j : 24 * j + 24, :].astype(BF16)
    to_seq(lambda o: dsl.at[o], lambda d: dslr.at[d - 1], 14, dslr)
    wait_bytes(nz.at[0:7], rsem.at[13])
    for j in range(8):
        nzs[:, 512 * j : 512 * j + 512] = nz[j].astype(F32)
    half = div(y, 2)
    slot = kv * 2 + rem(y, 2)
    nbo[...] = nzs[...].astype(BF16)

    @pl.loop(0, 16)
    def _(d):
        q = rem(x * 4 + y + d, 16)
        target = 2 * div(q, 4) + half
        to_me = (d == 0) & (half == core)

        @pl.when(jnp.logical_not(to_me))
        def _():
            send(nbo, nb.at[slot], ssem.at[15], rsem.at[15], {"kv": target, "vocab": rem(q, 4)})

        @pl.when(to_me)
        def _():
            pltpu.make_async_copy(nbo, nb.at[slot], rsem.at[15]).start()

    sent.append((nb.at[0:15], 15))
    wait_bytes(dslr, rsem.at[14])
    for i in range(4):
        lifted = dsl[z, i].astype(F32)
        for j in range(7):
            lifted = lifted + dslr[j, i].astype(F32)
        lifted = lifted + biasf[i : i + 1, :]
        zbo[i] = (lifted / (1.0 + jnp.exp(-lifted))).astype(BF16)
    reader = 2 * x + div(z, 4)
    landing = zb.at[core, rem(z, 4)]
    for d in range(8):
        other = rem(z + d, 8)
        if d:
            send(zbo, landing, ssem.at[16], rsem.at[16], {"kv": reader, "seq": other})
    keep = core == div(z, 4)

    @pl.when(jnp.logical_not(keep))
    def _():
        send(zbo, landing, ssem.at[16], rsem.at[16], {"kv": sibling})

    @pl.when(keep)
    def _():
        pltpu.make_async_copy(zbo, landing, rsem.at[16]).start()

    sent.append((zb.at[0, 0:4], 16))
    sent.append((zb.at[0, 0:3], 16))
    wait_bytes(zb, rsem.at[16])

    def block(s, o, t, part=None):
        bx, by = (x + o, y + t) if s == 0 else (x + t, y + o)
        at = pl.multiple_of(((2 * rem(bx + 4, 4) + s) * 4 + rem(by + 4, 4)) * 128, 128)
        if part is None:
            return big.at[:, :, pl.ds(at, 128)]
        return big.at[2 * part : 2 * part + 2, :, pl.ds(at, 128)]

    def neighbour(axis, step):
        if axis == 0:
            return {"kv": rem(kv + 2 * step + 8, 8)}
        return {"vocab": rem(y + step + 4, 4)}

    def ring(ref, s, axis, step, sem):
        send(ref, ref, sring.at[s], sem, neighbour(axis, step))

    offsets = (0, -1, 1, 2)

    def second_axis(s, oi):
        ref = block(s, offsets[oi], 0)
        ring(ref, s, 1 - s, 1, r2.at[s, oi, 0])
        ring(ref, s, 1 - s, -1, r2.at[s, oi, 1])

    def pass_on(s, oi):
        wait_bytes(block(s, 0, 0), r2.at[s, oi, 0])
        ring(block(s, offsets[oi], -1, 0), s, 1 - s, 1, r2h.at[s, oi, 0])
        wait_bytes(block(s, 0, 0), r2.at[s, oi, 1])
        ring(block(s, offsets[oi], 1, 1), s, 1 - s, -1, r2h.at[s, oi, 1])

    for s in range(2):
        for i in range(4):
            for j in range(4):
                bf[i, 24 * j : 24 * j + 24, :] = zb[s, j, i].astype(F32)
        own = block(s, 0, 0)
        for i in range(4):
            own[i] = bf[i].astype(BF16)
        ring(own, s, s, 1, r1.at[s, 0])
        ring(own, s, s, -1, r1.at[s, 1])
        second_axis(s, 0)

    mine = ((kv * 8 + z) * 4 + y) * 512
    theirs = ((sibling * 8 + z) * 4 + y) * 512

    def score(raw, ids, acc, lanes, i):
        logits = LOGIT_CAP * jnp.tanh(raw * (1.0 / LOGIT_CAP))
        entry = iota(raw.shape, 0)
        wanted = ids - (mine + 256 * i if i < 2 else theirs + 256 * (i - 2))
        for c in range(8):
            hit = entry == wanted[c : c + 1, :]
            acc[c : c + 1, 0:lanes] += jnp.sum(jnp.where(hit, logits, 0.0), axis=0, keepdims=True)
        acc[8:9, 0:lanes] += jnp.sum(jnp.exp(logits), axis=0, keepdims=True)

    def base(i):
        raw = dot_nt(wp[256 * i : 256 * i + 256, :], bbase[...])
        for d in range(4):
            base4[256 * i : 256 * i + 256, 96 * d : 96 * d + 96] = raw
        score(raw, tokb[:, 0:96], accb, 96, i)

    p96 = get("p96")
    for s in range(2):
        wait_bytes(block(s, 0, 0), r1.at[s, 0])
        ring(block(s, -1, 0, 0), s, s, 1, r1.at[s, 2])
        second_axis(s, 1)
    for s in range(2):
        wait_bytes(block(s, 0, 0), r1.at[s, 1])
        ring(block(s, 1, 0, 1), s, s, -1, r1.at[s, 3])
        second_axis(s, 2)
    for s in range(2):
        pass_on(s, 0)
    for s in range(2):
        wait_bytes(block(s, 0, 0, 0), r1.at[s, 2])
        wait_bytes(block(s, 0, 0, 1), r1.at[s, 3])
        second_axis(s, 3)
    wait_bytes(nb, rsem.at[15])
    for t in range(16):
        basef[8 * t : 8 * t + 8, :] = nb[t].astype(F32)
    bbase[...] = dot(p96[...], basef[...].astype(BF16)).astype(BF16)
    wait_bytes(wp.at[0:512], rsem.at[17])
    base(0)
    for s in range(2):
        pass_on(s, 1)
    base(1)
    for s in range(2):
        pass_on(s, 2)
    base(2)
    for s in range(2):
        pass_on(s, 3)
    base(3)
    for s in range(2):
        for oi in range(4):
            wait_bytes(block(s, 0, 0, 0), r2h.at[s, oi, 0])
            wait_bytes(block(s, 0, 0, 1), r2h.at[s, oi, 1])

    for i in range(4):
        rows = slice(256 * i, 256 * i + 256)
        raw = dot_nt(wp[rows, :], big[...].reshape(384, 4096)) + base4[rows, :]
        score(raw, tokd[...], accd, 384, i)

    rz[:, 0:128] = accb[...].astype(BF16)
    rz[:, 128:512] = accd[...].astype(BF16)
    to_seq(lambda o: rz, lambda d: rzr.at[d - 1], 18, rzr)
    wait_bytes(rzr, rsem.at[18])
    res = rz[...].astype(F32)
    for j in range(7):
        res = res + rzr[j].astype(F32)
    rp[p] = res.astype(BF16)
    to_plane(lambda q: rp.at[p], lambda d: rp.at[p], 19, rp.at[0:31])
    wait_bytes(rp.at[0:31], rsem.at[19])
    for c in range(2):
        res = jnp.zeros((16, 512), F32)
        for x4 in range(4):
            for yy in range(4):
                res = res + rp[(2 * x4 + c) * 4 + yy].astype(F32)
        res_ref[c] = res

    for ref, s in sent:
        wait_bytes(ref, ssem.at[s])

    @pl.when(half != core)
    def _():
        wait_bytes(nbo, ssem.at[15])

    @pl.when(jnp.logical_not(keep))
    def _():
        wait_bytes(zbo, ssem.at[16])

    for s in range(2):
        wait_bytes(big.at[:, :, 0:1920], sring.at[s])


def emit_kernel(
    len_ref, path_ref, kn_ref, vn_ref, res_ref, keys_ref, values_ref,
    keys_out, values_out, logn_ref, pick_ref,
):
    step = pl.program_id(0)
    rows = keys_ref.shape[0]
    length = len_ref[0]
    start = lax.axis_index("seq") * (rows * pl.num_programs(0)) + step * rows
    keys = keys_ref[...]
    values = values_ref[...]
    keys_out[...] = keys
    values_out[...] = values

    @pl.when((start + rows > length) & (start < length + 5))
    def _():
        away = start + iota((rows, 1), 0) - length
        target = jnp.full((rows, 1), -1, jnp.int32)
        for a in range(5):
            target = jnp.where(away == a, path_ref[0, a], target)
        selector = jnp.where(iota((rows, 48), 1) == target, 1.0, 0.0).astype(BF16)
        inside = jnp.broadcast_to(target, (rows, 256)) >= 0
        for fresh, old, out in ((kn_ref, keys, keys_out), (vn_ref, values, values_out)):
            out[...] = jnp.where(inside, dot(selector, fresh[...]), old.astype(F32)).astype(BF16)

    @pl.when(step == 0)
    def _():
        for c in range(2):
            logs = jnp.log(res_ref[c, 8:9, :])
            for n in range(5):
                for k in range(2):
                    lane = 48 * k if n == 0 else 128 + 96 * (n - 1) + 48 * k
                    logn_ref[n, 2 * c + k : 2 * c + k + 1, :] = logs[:, lane : lane + 48]
                    pick_ref[n, 2 * c + k] = res_ref[c, 0:8, lane : lane + 48]


def one_hot_rows(rows, columns, places):
    table = np.zeros((rows, columns), np.float32)
    table[np.arange(rows), places] = 1.0
    return table


def tables():
    r48 = np.arange(48)
    p48 = one_hot_rows(48, 64, (r48 // 6) * 8 + r48 % 6)
    r192 = np.arange(192)
    tenant, node = r192 // 48, r192 % 48
    p192 = one_hot_rows(192, 256, ((node // 6) * 4 + tenant) * 8 + node % 6)
    r96 = np.arange(96)
    tenant, node = r96 // 48, r96 % 48
    p96 = one_hot_rows(96, 128, ((node // 6) * 2 + tenant) * 8 + node % 6)
    return p48, p192, p96


def vmem(shape, dtype=BF16):
    return pltpu.VMEM(shape, dtype)


VM = pl.BlockSpec(memory_space=pltpu.VMEM)
SM = pl.BlockSpec(memory_space=pltpu.SMEM)
ANY = pl.BlockSpec(memory_space=pl.ANY)
DMA = pltpu.SemaphoreType.DMA


HBM = pl.BlockSpec(memory_space=pltpu.HBM)


def local(
    hidden_state,
    input_projection,
    output_projection,
    norm_pre_attention,
    norm_post_attention,
    norm_pre_feedforward,
    norm_post_feedforward,
    norm_final,
    cache_keys,
    cache_values,
    cache_length,
    ancestors,
    accepted_path,
    gate_up_weight,
    down_weight,
    draft_weight,
    draft_bias,
    vocab_weight,
    candidate_tokens,
):
    p48, p192, p96 = (jnp.asarray(t, BF16) for t in tables())
    frequency = jnp.asarray(
        (10000.0 ** (-2.0 * np.arange(128, dtype=np.float64) / 256)).astype(np.float32)
    )
    slots = cache_keys.shape[1]
    keys = cache_keys.reshape(slots, 256)
    values = cache_values.reshape(slots, 256)
    arrays = dict(
        h=hidden_state.reshape(6, 448),
        p48=p48,
        g_att=norm_pre_attention.reshape(1, 448),
        w_in=input_projection.reshape(448, 1024),
        freq=frequency.reshape(1, 128),
        anc=ancestors[0],
        keys=keys,
        values=values,
        e64=p48.T,
        w_out=output_projection[0].T,
        g_post=norm_post_attention.reshape(1, 448),
        g_pre=norm_pre_feedforward.reshape(1, 448),
        p192=p192,
        w_gu=gate_up_weight.reshape(448, 896),
        e256=p192.T,
        w_down=down_weight,
        g_fpost=norm_post_feedforward.reshape(1, 448),
        g_fin=norm_final.reshape(1, 448),
        w_draft=draft_weight,
        bias=draft_bias,
        cand=jnp.transpose(candidate_tokens, (0, 2, 3, 1)),
        p96=p96,
        w_voc=vocab_weight,
    )
    operands = [arrays[name] for name in LOADS]
    new_keys, new_values, result = pl.pallas_call(
        step_kernel,
        name="step",
        out_shape=(
            jax.ShapeDtypeStruct((48, 256), BF16),
            jax.ShapeDtypeStruct((48, 256), BF16),
            jax.ShapeDtypeStruct((2, 16, 512), F32),
        ),
        in_specs=[SM] + [HBM] * len(LOADS),
        out_specs=(VM, VM, VM),
        scratch_shapes=[vmem(a.shape, a.dtype) for a in operands] + [
            vmem((1024, 4096)), vmem((896, 1024)), vmem((8, 448), F32), vmem((8, 8, 448)),
            vmem((64, 448), F32), vmem((8, 64, 128)), vmem((7, 64, 128)), vmem((8, 48, 128)),
            vmem((96, 256)),
            vmem((96, 1), F32), vmem((96, 256), F32), vmem((8, 40, 128)), vmem((7, 40, 128)),
            vmem((8, 24, 128)), vmem((48, 512), F32), vmem((8, 8, 448)), vmem((7, 8, 448)),
            vmem((8, 128), F32), vmem((7, 8, 128), F32), vmem((32, 8, 448)), vmem((256, 448), F32),
            vmem((8, 24, 896)), vmem((7, 24, 896)), vmem((8, 24, 448)), vmem((192, 448), F32),
            vmem((32, 8, 448)), vmem((31, 8, 448)),
            vmem((8, 128), F32), vmem((7, 8, 128), F32), vmem((32, 8, 448)), vmem((8, 8, 512)),
            vmem((8, 4096), F32), vmem((8, 4096)), vmem((16, 8, 4096)),
            vmem((4, 192, 128), F32), vmem((8, 4, 24, 128)), vmem((7, 4, 24, 128)),
            vmem((8, 128), F32), vmem((4, 24, 128)), vmem((2, 4, 4, 24, 128)),
            vmem((4, 96, 128), F32), vmem((4, 96, 4096)), vmem((128, 4096), F32), vmem((96, 4096)),
            vmem((1024, 384), F32), vmem((8, 128), jnp.int32), vmem((8, 384), jnp.int32),
            vmem((16, 512)), vmem((7, 16, 512)), vmem((32, 16, 512)),
            vmem((16, 128), F32), vmem((16, 384), F32),
            DMA((len(LOADS),)), DMA((20,)), DMA((20,)), DMA((2,)), DMA((2, 4)), DMA((2, 4, 2)),
            DMA((2, 4, 2)),
        ],
        compiler_params=pltpu.CompilerParams(
            collective_id=0, has_side_effects=True, vmem_limit_bytes=62 << 20
        ),
    )(cache_length, *operands)
    block = 512
    rowspec = pl.BlockSpec((block, 256), lambda i: (i, 0))

    def whole(shape):
        return pl.BlockSpec(shape, lambda i: (0,) * len(shape))

    keys_updated, values_updated, log_normalizer, picked = pl.pallas_call(
        emit_kernel,
        name="emit",
        grid=(slots // block,),
        out_shape=(
            jax.ShapeDtypeStruct((slots, 256), BF16),
            jax.ShapeDtypeStruct((slots, 256), BF16),
            jax.ShapeDtypeStruct((5, 4, 48), F32),
            jax.ShapeDtypeStruct((5, 4, 8, 48), F32),
        ),
        in_specs=[
            SM, SM, whole((48, 256)), whole((48, 256)), whole((2, 16, 512)), rowspec, rowspec,
        ],
        out_specs=(rowspec, rowspec, whole((5, 4, 48)), whole((5, 4, 8, 48))),
        compiler_params=pltpu.CompilerParams(vmem_limit_bytes=62 << 20),
    )(cache_length, accepted_path, new_keys, new_values, result, keys, values)
    return (
        keys_updated.reshape(cache_keys.shape),
        values_updated.reshape(cache_values.shape),
        jnp.transpose(log_normalizer, (0, 2, 1)),
        jnp.transpose(picked, (0, 3, 1, 2)),
    )


def solution(mesh):
    placed = (
        P("kv", "vocab", "seq"),
        P("seq", "kv", None),
        P("kv", None, "seq"),
        P("seq"),
        P("seq"),
        P("seq"),
        P("seq"),
        P("seq"),
        P("vocab", "seq", "kv", None),
        P("vocab", "seq", "kv", None),
        P("vocab"),
        P("vocab", None, None),
        P("vocab", None),
        P("seq", None, ("kv", "vocab")),
        P(("kv", "vocab"), "seq"),
        P(None, "seq", ("kv", "vocab")),
        P(None, ("kv", "vocab")),
        P(("kv", "seq", "vocab"), None),
        P(),
    )
    return jax.shard_map(
        local,
        mesh=mesh,
        in_specs=placed,
        out_specs=(P("vocab", "seq", "kv", None), P("vocab", "seq", "kv", None), P(), P()),
        check_vma=False,
    )
```

```python
import jax
import jax.numpy as jnp
import numpy as np
from jax import lax
from jax.experimental import pallas as pl
from jax.experimental.pallas import tpu as pltpu
from jax.sharding import PartitionSpec as P

MESH = pl.DeviceIdType.MESH
F32 = jnp.float32
BF16 = jnp.bfloat16
WIDTH = 3584
EPSILON = 1e-06
SCORE_CAP = 50.0
LOGIT_CAP = 30.0
NT = (((1,), (1,)), ((), ()))


def rem(a, n):
    return lax.rem(a, jnp.int32(n))


def div(a, n):
    return lax.div(a, jnp.int32(n))


def dot(a, b):
    return jnp.dot(a, b, preferred_element_type=F32)


def dot_nt(a, b):
    return lax.dot_general(a, b, NT, preferred_element_type=F32)


def iota(shape, dim):
    return lax.broadcasted_iota(jnp.int32, shape, dim)


def send(src, dst, ssem, rsem, peer):
    pltpu.make_async_remote_copy(
        src_ref=src,
        dst_ref=dst,
        send_sem=ssem,
        recv_sem=rsem,
        device_id=peer,
        device_id_type=MESH,
    ).start()


def wait_bytes(ref, sem):
    pltpu.make_async_copy(ref, ref, sem).wait()


def plane_peer(p, d):
    q = rem(p + d, 32)
    return q, {"kv": div(q, 4), "vocab": rem(q, 4)}


def position_in_mesh():
    return lax.axis_index("kv"), lax.axis_index("seq"), lax.axis_index("vocab")


def capped_weight(scores):
    return jnp.exp(SCORE_CAP * jnp.tanh(scores * (0.0625 / SCORE_CAP)))


def moments(values):
    lane = iota((8, 128), 1)
    tile = jnp.zeros((8, 128), F32)
    for i, v in enumerate(values):
        tile = jnp.where(lane == i, jnp.sum(v, axis=1, keepdims=True), tile)
    return tile


def rms_inverse(total):
    return lax.rsqrt(jnp.maximum(total, 0.0) / WIDTH + EPSILON)


LOADS = (
    "h", "p48", "g_att", "w_in", "freq", "anc", "keys", "values", "e64", "w_out", "g_post",
    "g_pre", "p192", "w_gu", "e256", "w_down", "g_fpost", "g_fin", "w_draft", "bias", "cand",
    "w_voc",
)


def step_kernel(len_ref, *refs):
    count = len(LOADS)
    source = dict(zip(LOADS, refs[:count]))
    kn, vn, res_ref = refs[count : count + 3]
    here = dict(zip(LOADS, refs[count + 3 : 2 * count + 3]))
    (
        wp, spread, pad8, xg, xf6, ps, prc, agc, qs,
        den, num, ns, nr, ga, af, os_, orr, ms, mr, fp, xf, gs, gr, ags, acts, ds, dsr,
        ms2, mr2, npl, nsc, nbz, lf, dsl, dslr, biasf, zbo, zb, bf, big, bbase,
        base4, tokb, tokd, rz, rx, ry, accb, accd,
        wgu, fin, wsem, ssem, rsem, zr, sring, r1, r2, r2h,
    ) = refs[2 * count + 3 :]
    kv, z, y = position_in_mesh()
    core = rem(kv, 2)
    x = div(kv, 2)
    p = kv * 4 + y
    sibling = kv + 1 - 2 * core
    barrier = pltpu.get_barrier_semaphore()

    @pl.loop(1, 32)
    def _(d):
        pl.semaphore_signal(barrier, inc=1, device_id=plane_peer(p, d)[1], device_id_type=MESH)

    for d in (4, 3, 5, 2, 6, 1, 7):
        other = rem(z + d, 8)
        pl.semaphore_signal(barrier, inc=1, device_id={"seq": other}, device_id_type=MESH)
        pl.semaphore_signal(barrier, inc=1, device_id={"kv": sibling, "seq": other}, device_id_type=MESH)
    copies = {}
    for i, name in enumerate(LOADS):
        copies[name] = pltpu.make_async_copy(source[name], here[name], wsem.at[i])
        copies[name].start()

    def get(name):
        copies[name].wait()
        return here[name]

    sent = []

    def to_seq(src, dst, s, total):
        for d in (4, 3, 5, 2, 6, 1, 7):
            other = rem(z + d, 8)
            send(src(other), dst(d), ssem.at[s], rsem.at[s], {"seq": other})
        sent.append((total, s))

    def to_kv(src, dst, s, total):
        for d in (4, 5, 3, 2, 6, 1, 7):
            other = rem(kv + d, 8)
            send(src(other), dst(d), ssem.at[s], rsem.at[s], {"kv": other})
        sent.append((total, s))

    def to_plane(src, dst, s, total):
        @pl.loop(0, 31)
        def _(i):
            d = rem(i + 14, 31) + 1
            q, peer = plane_peer(p, d)
            send(src(q), dst(d), ssem.at[s], rsem.at[s], peer)

        sent.append((total, s))

    pad8[...] = jnp.zeros_like(pad8)
    pad8[0:6, :] = get("h")[...].astype(F32)
    xg[kv] = pad8[...].astype(BF16)
    pl.semaphore_wait(barrier, 45)
    to_kv(lambda o: xg.at[kv], lambda d: xg.at[kv], 0, xg.at[0:7])
    depth = jnp.sum(get("anc")[...].astype(F32), axis=1, keepdims=True) - 1.0
    angle = (len_ref[0].astype(F32) + depth) * get("freq")[...]
    cosine = jnp.cos(angle)
    sine = jnp.sin(angle)
    eye = iota((96, 128), 0) == iota((96, 128), 1)
    p48 = get("p48")
    gain = get("g_att")[...]
    w_in = get("w_in")
    wait_bytes(xg.at[0:7], rsem.at[0])
    for j in range(8):
        xf6[8 * j : 8 * j + 8, :] = xg[j].astype(F32)
    tokens = dot(p48[...], xf6[...].astype(BF16))
    squares = jnp.sum(tokens * tokens, axis=1, keepdims=True)
    row = jnp.sum(jnp.where(eye[0:48], squares, 0.0), axis=0, keepdims=True)
    row = jnp.broadcast_to(row, (8, 128)).astype(BF16)
    part = dot((tokens * gain).astype(BF16), w_in[...])
    for j in range(8):
        ps[j, 0:48, :] = part[:, 128 * j : 128 * j + 128].astype(BF16)
        ps[j, 48:56, :] = row
    to_seq(lambda o: ps.at[o], lambda d: prc.at[d - 1], 1, prc)
    lane = iota((896, 1024), 1)
    inside = lane & 127
    place = lax.shift_right_logical(lane, 7) * 112 + inside
    spread[...] = jnp.where((iota((896, 1024), 0) == place) & (inside < 112), 1.0, 0.0).astype(BF16)
    wait_bytes(prc, rsem.at[1])
    chunk = ps[z].astype(F32)
    for j in range(7):
        chunk = chunk + prc[j].astype(F32)
    column = jnp.sum(jnp.where(eye[0:48], chunk[48:49, :], 0.0), axis=1, keepdims=True)
    agc[z] = (chunk[0:48] * rms_inverse(column)).astype(BF16)
    to_seq(lambda o: agc.at[z], lambda d: agc.at[z], 2, agc.at[0:7])
    keys, values = get("keys"), get("values")
    wait_bytes(agc.at[0:7], rsem.at[2])
    for j, (ref, row0) in enumerate(((qs, 0), (qs, 48), (kn, 0))):
        first = agc[2 * j].astype(F32)
        second = agc[2 * j + 1].astype(F32)
        ref[row0 : row0 + 48, 0:128] = (first * cosine - second * sine).astype(BF16)
        ref[row0 : row0 + 48, 128:256] = (second * cosine + first * sine).astype(BF16)
    vn[:, 0:128] = agc[6]
    vn[:, 128:256] = agc[7]

    queries = qs[...]
    anc = jnp.where(z == 0, here["anc"][...], 0)
    anc = jnp.concatenate([anc, anc], axis=0)
    weights = capped_weight(dot_nt(queries, kn[...]))
    weights = jnp.where(anc > 0, weights, 0.0)
    den[...] = jnp.sum(weights, axis=1, keepdims=True)
    num[...] = dot(weights.astype(BF16), vn[...])
    filled = len_ref[0] - z * 2048

    @pl.loop(0, 4)
    def _(i):
        rows = pl.ds(pl.multiple_of(i * 512, 512), 512)
        weights = capped_weight(dot_nt(queries, keys[rows, :]))
        weights = jnp.where(iota((96, 512), 1) < filled - i * 512, weights, 0.0)
        den[...] += jnp.sum(weights, axis=1, keepdims=True)
        num[...] += dot(weights.astype(BF16), values[rows, :])

    row = jnp.sum(jnp.where(eye, den[...], 0.0), axis=0, keepdims=True)
    row = jnp.broadcast_to(row, (16, 128)).astype(BF16)
    for j in range(8):
        r0, c0 = 24 * (j // 2), 128 * (j % 2)
        ns[j, 0:16, :] = row
        ns[j, 16:40, :] = num[r0 : r0 + 24, c0 : c0 + 128].astype(BF16)
    to_seq(lambda o: ns.at[o], lambda d: nr.at[d - 1], 3, nr)
    raw_gu = get("w_gu")

    def relay_out(i):
        rows = slice(112 * i, 112 * i + 112)
        wgu[rows, 0:448] = raw_gu[rows, 0, :]
        wgu[rows, 448:896] = raw_gu[rows, 1, :]

    relay_out(0)
    relay_out(1)
    e64, w_out = get("e64"), get("w_out")
    wait_bytes(nr, rsem.at[3])
    total = ns[z].astype(F32)
    for j in range(7):
        total = total + nr[j].astype(F32)
    chosen = iota((24, 128), 1) == iota((24, 128), 0) + 24 * div(z, 2)
    below = jnp.sum(jnp.where(chosen, total[0:1, :], 0.0), axis=1, keepdims=True)
    ga[z] = (total[16:40, :] / below).astype(BF16)
    to_seq(lambda o: ga.at[z], lambda d: ga.at[z], 4, ga.at[0:7])
    relay_out(2)
    relay_out(3)
    w_voc = get("w_voc")

    def widen(j):
        wp[0:512, 1024 * j : 1024 * j + 1024] = dot(
            w_voc[:, 896 * j : 896 * j + 896], spread[...]
        ).astype(BF16)

    wait_bytes(ga.at[0:7], rsem.at[4])
    for j in range(8):
        r0, c0 = 24 * ((j // 2) % 2), 256 * (j // 4) + 128 * (j % 2)
        af[r0 : r0 + 24, c0 : c0 + 128] = ga[j].astype(F32)
    attended = dot(e64[...], af[...].astype(BF16)).astype(BF16)
    out = dot_nt(attended, w_out[...])
    for j in range(8):
        os_[j] = out[8 * j : 8 * j + 8, :].astype(BF16)
    to_kv(lambda o: os_.at[o], lambda d: orr.at[d - 1], 5, orr)
    hidden = pad8[...]
    gain = get("g_post")[...]
    wait_bytes(orr, rsem.at[5])
    att = os_[kv].astype(F32)
    for j in range(7):
        att = att + orr[j].astype(F32)
    gained = att * gain
    ms[...] = moments((att * att, hidden * gained, gained * gained, hidden * hidden))
    to_seq(lambda o: ms, lambda d: mr.at[d - 1], 6, mr)
    gain = get("g_pre")[...]
    wait_bytes(mr, rsem.at[6])
    tot = ms[...]
    for j in range(7):
        tot = tot + mr[j]
    inv = rms_inverse(tot[:, 0:1])
    first = (hidden + gained * inv).astype(BF16).astype(F32)
    inv = rms_inverse(tot[:, 3:4] + 2.0 * inv * tot[:, 1:2] + inv * inv * tot[:, 2:3])
    fp[p] = (first * inv * gain).astype(BF16)
    to_plane(lambda q: fp.at[p], lambda d: fp.at[p], 7, fp.at[0:31])
    widen(0)
    p192 = get("p192")
    wait_bytes(fp.at[0:31], rsem.at[7])
    for j in range(32):
        xf[8 * j : 8 * j + 8, :] = fp[j].astype(F32)
    rows192 = dot(p192[...], xf[...].astype(BF16)).astype(BF16)
    gu = dot(rows192, wgu[...])
    for j in range(8):
        gs[j] = gu[24 * j : 24 * j + 24, :].astype(BF16)
    to_seq(lambda o: gs.at[o], lambda d: gr.at[d - 1], 8, gr)
    widen(1)
    widen(2)
    widen(3)
    send(wp.at[0:512], wp.at[512:1024], ssem.at[17], rsem.at[17], {"kv": sibling})
    sent.append((wp.at[0:512], 17))
    e256, w_down = get("e256"), get("w_down")
    wait_bytes(gr, rsem.at[8])
    gu = gs[z].astype(F32)
    for j in range(7):
        gu = gu + gr[j].astype(F32)
    gate, up = gu[:, 0:448], gu[:, 448:896]
    gelu = 0.5 * gate * (1.0 + jnp.tanh(0.7978845608028654 * (gate + 0.044715 * gate * gate * gate)))
    ags[z] = (gelu * up).astype(BF16)
    to_seq(lambda o: ags.at[z], lambda d: ags.at[z], 9, ags.at[0:7])
    cand = get("cand")
    for n in range(5):
        for k in range(2):
            ids = cand[n, 2 * core + k]
            if n == 0:
                tokb[:, 48 * k : 48 * k + 48] = ids
            else:
                at = 96 * (n - 1) + 48 * k
                tokd[:, at : at + 48] = ids
    lf[...] = jnp.zeros_like(lf)
    biasf[...] = jnp.zeros_like(biasf)
    biasf[0:4, 0:112] = get("bias")[...]
    accb[...] = jnp.zeros_like(accb)
    base4[...] = jnp.zeros_like(base4)
    accd[...] = jnp.zeros_like(accd)
    wait_bytes(ags.at[0:7], rsem.at[9])
    for j in range(8):
        acts[24 * j : 24 * j + 24, :] = ags[j].astype(F32)
    act = dot(e256[...], acts[...].astype(BF16)).astype(BF16)
    out = dot(act, w_down[...])
    for j in range(32):
        ds[j] = out[8 * j : 8 * j + 8, :].astype(BF16)
    to_plane(lambda q: ds.at[q], lambda d: dsr.at[d - 1], 10, dsr)
    gain = get("g_fpost")[...]
    wait_bytes(dsr, rsem.at[10])
    out = ds[p].astype(F32)
    for j in range(31):
        out = out + dsr[j].astype(F32)
    gained = out * gain
    ms2[...] = moments((out * out, first * gained, gained * gained, first * first))
    to_seq(lambda o: ms2, lambda d: mr2.at[d - 1], 11, mr2)
    gain = get("g_fin")[...]
    w_draft = get("w_draft")
    wait_bytes(mr2, rsem.at[11])
    tot = ms2[...]
    for j in range(7):
        tot = tot + mr2[j]
    inv = rms_inverse(tot[:, 0:1])
    second = (first + gained * inv).astype(BF16).astype(F32)
    inv = rms_inverse(tot[:, 3:4] + 2.0 * inv * tot[:, 1:2] + inv * inv * tot[:, 2:3])
    normed = (second * inv * gain).astype(BF16)
    npl[p] = normed
    to_plane(lambda q: npl.at[p], lambda d: npl.at[p], 12, npl.at[0:31])
    wait_bytes(npl.at[0:31], rsem.at[12])
    for j in range(32):
        xf[8 * j : 8 * j + 8, :] = npl[j].astype(F32)
    rows192 = dot(p192[...], xf[...].astype(BF16)).astype(BF16)
    halves = (slice(0, 2), slice(2, 4))
    for h, (lifted_sem, pair) in enumerate(((13, halves[0]), (14, halves[1]))):
        for i in (2 * h, 2 * h + 1):
            lf[i, :, 0:112] = dot(rows192, w_draft[i])
            for j in range(8):
                dsl[j, i] = lf[i, 24 * j : 24 * j + 24, :].astype(BF16)
        to_seq(
            lambda o: dsl.at[o, pair], lambda d: dslr.at[d - 1, pair], lifted_sem, dslr.at[:, pair]
        )
    nsc[0] = rows192[0:96]
    nsc[1] = rows192[96:192]
    reader = 2 * x + div(z, 4)
    keep = core == div(z, 4)
    for h, (lifted_sem, group_sem, pair) in enumerate(((13, 16, halves[0]), (14, 20, halves[1]))):
        wait_bytes(dslr.at[:, pair], rsem.at[lifted_sem])
        for i in (2 * h, 2 * h + 1):
            lifted = dsl[z, i].astype(F32)
            for j in range(7):
                lifted = lifted + dslr[j, i].astype(F32)
            lifted = lifted + biasf[i : i + 1, :]
            zbo[i] = (lifted / (1.0 + jnp.exp(-lifted))).astype(BF16)
        mine, landing = zbo.at[pair], zb.at[core, rem(z, 4), pair]
        for d in (4, 3, 5, 2, 6, 1, 7):
            send(mine, landing, ssem.at[group_sem], rsem.at[group_sem], {"kv": reader, "seq": rem(z + d, 8)})

        @pl.when(jnp.logical_not(keep))
        def _():
            send(mine, landing, ssem.at[group_sem], rsem.at[group_sem], {"kv": sibling})

        @pl.when(keep)
        def _():
            pltpu.make_async_copy(mine, landing, rsem.at[group_sem]).start()

        sent.append((zb.at[0, 0:4, pair], group_sem))
        sent.append((zb.at[0, 0:3, pair], group_sem))
    nbz[z] = nsc[core]

    def along_seq(ref, step, sem):
        send(ref, ref, ssem.at[15], sem, {"seq": rem(z + step + 8, 8)})

    sent.append((nbz.at[0:7], 15))
    along_seq(nbz.at[z], 1, zr.at[0, 0])
    along_seq(nbz.at[z], -1, zr.at[0, 1])

    def base_on(k):
        wait_bytes(nbz.at[0], zr.at[k - 1, 0])
        left = nbz.at[rem(z - k + 8, 8)]
        along_seq(left if k < 3 else left.at[0:48], 1, zr.at[k, 0])
        wait_bytes(nbz.at[0], zr.at[k - 1, 1])
        right = nbz.at[rem(z + k, 8)]
        along_seq(right if k < 3 else right.at[48:96], -1, zr.at[k, 1])

    def block(h, s, o, t, part=None):
        bx, by = (x + o, y + t) if s == 0 else (x + t, y + o)
        at = pl.multiple_of(((2 * rem(bx + 4, 4) + s) * 4 + rem(by + 4, 4)) * 128, 128)
        if part is None:
            return big.at[2 * h : 2 * h + 2, :, pl.ds(at, 128)]
        return big.at[2 * h + part : 2 * h + part + 1, :, pl.ds(at, 128)]

    def neighbour(axis, step):
        if axis == 0:
            return {"kv": rem(kv + 2 * step + 8, 8)}
        return {"vocab": rem(y + step + 4, 4)}

    def ring(ref, s, axis, step, sem):
        send(ref, ref, sring.at[s], sem, neighbour(axis, step))

    offsets = (0, -1, 1, 2)

    def second_axis(h, s, oi):
        ref = block(h, s, offsets[oi], 0)
        ring(ref, s, 1 - s, 1, r2.at[h, s, oi, 0])
        ring(ref, s, 1 - s, -1, r2.at[h, s, oi, 1])

    def pass_on(h, s, oi):
        wait_bytes(block(h, s, 0, 0), r2.at[h, s, oi, 0])
        ring(block(h, s, offsets[oi], -1, 0), s, 1 - s, 1, r2h.at[h, s, oi, 0])
        wait_bytes(block(h, s, 0, 0), r2.at[h, s, oi, 1])
        ring(block(h, s, offsets[oi], 1, 1), s, 1 - s, -1, r2h.at[h, s, oi, 1])

    both = tuple((h, s) for h in range(2) for s in range(2))
    for h, (group_sem, pair) in enumerate(((16, halves[0]), (20, halves[1]))):
        wait_bytes(zb.at[:, :, pair], rsem.at[group_sem])
        for s in range(2):
            own = block(h, s, 0, 0)
            for i in range(2):
                for j in range(4):
                    bf[i, 24 * j : 24 * j + 24, :] = zb[s, j, 2 * h + i].astype(F32)
                own[i] = bf[i].astype(BF16)
            ring(own, s, s, 1, r1.at[h, s, 0])
            ring(own, s, s, -1, r1.at[h, s, 1])
            second_axis(h, s, 0)

    mine = ((kv * 8 + z) * 4 + y) * 512
    theirs = ((sibling * 8 + z) * 4 + y) * 512

    def score(raw, ids, acc, lanes, i):
        logits = LOGIT_CAP * jnp.tanh(raw * (1.0 / LOGIT_CAP))
        entry = iota(raw.shape, 0)
        wanted = ids - (mine + 256 * i if i < 2 else theirs + 256 * (i - 2))
        for c in range(8):
            hit = entry == wanted[c : c + 1, :]
            acc[c : c + 1, 0:lanes] += jnp.sum(jnp.where(hit, logits, 0.0), axis=0, keepdims=True)
        acc[8:9, 0:lanes] += jnp.sum(jnp.exp(logits), axis=0, keepdims=True)

    def base(i):
        raw = dot_nt(wp[256 * i : 256 * i + 256, :], bbase[...])
        for d in range(4):
            base4[256 * i : 256 * i + 256, 96 * d : 96 * d + 96] += raw
        score(raw, tokb[:, 0:96], accb, 96, i)

    def add_columns(s, bx):
        at = pl.ds(pl.multiple_of((2 * rem(bx + 4, 4) + s) * 512, 512), 512)
        fresh = big[:, :, at].reshape(384, 512)
        for i in range(4):
            rows = slice(256 * i, 256 * i + 256)
            base4[rows, :] += dot_nt(wp[rows, at], fresh)

    def last_halves(s, oi):
        for h in range(2):
            wait_bytes(block(h, s, 0, 0, 0), r2h.at[h, s, oi, 0])
            wait_bytes(block(h, s, 0, 0, 1), r2h.at[h, s, oi, 1])

    for h, s in both:
        wait_bytes(block(h, s, 0, 0), r1.at[h, s, 0])
        ring(block(h, s, -1, 0, 0), s, s, 1, r1.at[h, s, 2])
        second_axis(h, s, 1)
        wait_bytes(block(h, s, 0, 0), r1.at[h, s, 1])
        ring(block(h, s, 1, 0, 1), s, s, -1, r1.at[h, s, 3])
        second_axis(h, s, 2)
    wait_bytes(wp.at[0:512], rsem.at[17])
    base_on(1)
    for h, s in both:
        pass_on(h, s, 0)
    for h, s in both:
        wait_bytes(block(h, s, 0, 0, 0), r1.at[h, s, 2])
        wait_bytes(block(h, s, 0, 0, 1), r1.at[h, s, 3])
        second_axis(h, s, 3)
    base_on(2)
    for h, s in both:
        pass_on(h, s, 1)
    add_columns(1, x)
    base_on(3)
    for h, s in both:
        pass_on(h, s, 2)
    last_halves(0, 0)
    add_columns(0, x)
    for h, s in both:
        pass_on(h, s, 3)
    wait_bytes(nbz.at[0, 0:48], zr.at[3, 0])
    wait_bytes(nbz.at[0, 0:48], zr.at[3, 1])
    for j in range(8):
        bbase[:, 512 * j : 512 * j + 512] = dot(nbz[j], spread[0:448, 0:512]).astype(BF16)
    for i in range(4):
        base(i)
    last_halves(0, 1)
    add_columns(0, x - 1)
    add_columns(1, x - 1)
    add_columns(1, x + 1)
    last_halves(0, 2)
    add_columns(0, x + 1)
    last_halves(0, 3)
    add_columns(0, x + 2)
    for oi in range(4):
        last_halves(1, oi)
    add_columns(1, x + 2)
    for i in range(4):
        score(base4[256 * i : 256 * i + 256, :], tokd[...], accd, 384, i)

    fin[...] = jnp.zeros_like(fin)
    fin[:, 0:96] = accb[0:8, 0:96]
    fin[:, 128:512] = accd[0:8, :]
    fin[0:1, 512:608] = accb[8:9, 0:96]
    for d in range(4):
        fin[d + 1 : d + 2, 512:608] = accd[8:9, 96 * d : 96 * d + 96]
    rz[z] = fin[...].astype(BF16)
    to_seq(lambda o: rz.at[z], lambda d: rz.at[z], 18, rz.at[0:7])
    wait_bytes(rz.at[0:7], rsem.at[18])

    def add_up(slots, count):
        res = slots[0].astype(F32)
        for j in range(1, count):
            res = res + slots[j].astype(F32)
        return res

    rx[x] = add_up(rz, 8).astype(BF16)
    for d in (2, 1, 3):
        send(rx.at[x], rx.at[x], ssem.at[19], rsem.at[19], {"kv": rem(kv + 2 * d, 8)})
    wait_bytes(rx.at[0:3], rsem.at[19])
    ry[core * 4 + y] = add_up(rx, 4).astype(BF16)
    place = ry.at[core * 4 + y]
    for d in (2, 1, 3, 0):
        other = rem(y + d, 4)
        send(place, place, ssem.at[21], rsem.at[21], {"kv": sibling, "vocab": other})
        if d:
            send(place, place, ssem.at[21], rsem.at[21], {"vocab": other})
    sent.append((rx.at[0:3], 19))
    sent.append((ry.at[0:7], 21))
    wait_bytes(ry.at[0:7], rsem.at[21])
    for c in range(2):
        res_ref[c] = add_up(ry.at[4 * c : 4 * c + 4], 4)

    for ref, s in sent:
        wait_bytes(ref, ssem.at[s])

    @pl.when(jnp.logical_not(keep))
    def _():
        wait_bytes(zbo.at[halves[0]], ssem.at[16])
        wait_bytes(zbo.at[halves[1]], ssem.at[20])

    for s in range(2):
        wait_bytes(big.at[:, :, 0:1920], sring.at[s])


def emit_kernel(
    len_ref, path_ref, kn_ref, vn_ref, res_ref, keys_ref, values_ref,
    keys_out, values_out, logn_ref, pick_ref,
):
    step = pl.program_id(0)
    rows = keys_ref.shape[0]
    length = len_ref[0]
    start = lax.axis_index("seq") * (rows * pl.num_programs(0)) + step * rows
    keys = keys_ref[...]
    values = values_ref[...]
    keys_out[...] = keys
    values_out[...] = values

    @pl.when((start + rows > length) & (start < length + 5))
    def _():
        away = start + iota((rows, 1), 0) - length
        target = jnp.full((rows, 1), -1, jnp.int32)
        for a in range(5):
            target = jnp.where(away == a, path_ref[0, a], target)
        selector = jnp.where(iota((rows, 48), 1) == target, 1.0, 0.0).astype(BF16)
        inside = jnp.broadcast_to(target, (rows, 256)) >= 0
        for fresh, old, out in ((kn_ref, keys, keys_out), (vn_ref, values, values_out)):
            out[...] = jnp.where(inside, dot(selector, fresh[...]), old.astype(F32)).astype(BF16)

    @pl.when(step == 0)
    def _():
        for c in range(2):
            for n in range(5):
                logs = jnp.log(res_ref[c, n : n + 1, 512:608])
                for k in range(2):
                    lane = 48 * k if n == 0 else 128 + 96 * (n - 1) + 48 * k
                    logn_ref[n, 2 * c + k : 2 * c + k + 1, :] = logs[:, 48 * k : 48 * k + 48]
                    pick_ref[n, 2 * c + k] = res_ref[c, 0:8, lane : lane + 48]


def one_hot_rows(rows, columns, places):
    table = np.zeros((rows, columns), np.float32)
    table[np.arange(rows), places] = 1.0
    return table


def tables():
    r48 = np.arange(48)
    p48 = one_hot_rows(48, 64, (r48 // 6) * 8 + r48 % 6)
    r192 = np.arange(192)
    tenant, node = r192 // 48, r192 % 48
    p192 = one_hot_rows(192, 256, ((node // 6) * 4 + tenant) * 8 + node % 6)
    return p48, p192


def vmem(shape, dtype=BF16):
    return pltpu.VMEM(shape, dtype)


VM = pl.BlockSpec(memory_space=pltpu.VMEM)
SM = pl.BlockSpec(memory_space=pltpu.SMEM)
ANY = pl.BlockSpec(memory_space=pl.ANY)
DMA = pltpu.SemaphoreType.DMA


HBM = pl.BlockSpec(memory_space=pltpu.HBM)


def local(
    hidden_state,
    input_projection,
    output_projection,
    norm_pre_attention,
    norm_post_attention,
    norm_pre_feedforward,
    norm_post_feedforward,
    norm_final,
    cache_keys,
    cache_values,
    cache_length,
    ancestors,
    accepted_path,
    gate_up_weight,
    down_weight,
    draft_weight,
    draft_bias,
    vocab_weight,
    candidate_tokens,
):
    p48, p192 = (jnp.asarray(t, BF16) for t in tables())
    frequency = jnp.asarray(
        (10000.0 ** (-2.0 * np.arange(128, dtype=np.float64) / 256)).astype(np.float32)
    )
    slots = cache_keys.shape[1]
    keys = cache_keys.reshape(slots, 256)
    values = cache_values.reshape(slots, 256)
    arrays = dict(
        h=hidden_state.reshape(6, 448),
        p48=p48,
        g_att=norm_pre_attention.reshape(1, 448),
        w_in=input_projection.reshape(448, 1024),
        freq=frequency.reshape(1, 128),
        anc=ancestors[0],
        keys=keys,
        values=values,
        e64=p48.T,
        w_out=output_projection[0].T,
        g_post=norm_post_attention.reshape(1, 448),
        g_pre=norm_pre_feedforward.reshape(1, 448),
        p192=p192,
        w_gu=gate_up_weight,
        e256=p192.T,
        w_down=down_weight,
        g_fpost=norm_post_feedforward.reshape(1, 448),
        g_fin=norm_final.reshape(1, 448),
        w_draft=draft_weight,
        bias=draft_bias,
        cand=jnp.transpose(candidate_tokens, (0, 2, 3, 1)),
        w_voc=vocab_weight,
    )
    operands = [arrays[name] for name in LOADS]
    new_keys, new_values, result = pl.pallas_call(
        step_kernel,
        name="step",
        out_shape=(
            jax.ShapeDtypeStruct((48, 256), BF16),
            jax.ShapeDtypeStruct((48, 256), BF16),
            jax.ShapeDtypeStruct((2, 8, 640), F32),
        ),
        in_specs=[SM] + [HBM] * len(LOADS),
        out_specs=(VM, VM, VM),
        scratch_shapes=[vmem(a.shape, a.dtype) for a in operands] + [
            vmem((1024, 4096)), vmem((896, 1024)), vmem((8, 448), F32), vmem((8, 8, 448)),
            vmem((64, 448), F32), vmem((8, 56, 128)), vmem((7, 56, 128)), vmem((8, 48, 128)),
            vmem((96, 256)),
            vmem((96, 1), F32), vmem((96, 256), F32), vmem((8, 40, 128)), vmem((7, 40, 128)),
            vmem((8, 24, 128)), vmem((48, 512), F32), vmem((8, 8, 448)), vmem((7, 8, 448)),
            vmem((8, 128), F32), vmem((7, 8, 128), F32), vmem((32, 8, 448)), vmem((256, 448), F32),
            vmem((8, 24, 896)), vmem((7, 24, 896)), vmem((8, 24, 448)), vmem((192, 448), F32),
            vmem((32, 8, 448)), vmem((31, 8, 448)),
            vmem((8, 128), F32), vmem((7, 8, 128), F32), vmem((32, 8, 448)),
            vmem((2, 96, 448)), vmem((8, 96, 448)),
            vmem((4, 192, 128), F32), vmem((8, 4, 24, 128)), vmem((7, 4, 24, 128)),
            vmem((8, 128), F32), vmem((4, 24, 128)), vmem((2, 4, 4, 24, 128)),
            vmem((2, 96, 128), F32), vmem((4, 96, 4096)), vmem((96, 4096)),
            vmem((1024, 384), F32), vmem((8, 128), jnp.int32), vmem((8, 384), jnp.int32),
            vmem((8, 8, 640)), vmem((4, 8, 640)), vmem((8, 8, 640)),
            vmem((16, 128), F32), vmem((16, 384), F32),
            vmem((448, 896)), vmem((8, 640), F32),
            DMA((len(LOADS),)), DMA((23,)), DMA((23,)), DMA((4, 2)), DMA((2,)), DMA((2, 2, 4)), DMA((2, 2, 4, 2)),
            DMA((2, 2, 4, 2)),
        ],
        compiler_params=pltpu.CompilerParams(
            collective_id=0, has_side_effects=True, vmem_limit_bytes=62 << 20
        ),
    )(cache_length, *operands)
    block = 512
    rowspec = pl.BlockSpec((block, 256), lambda i: (i, 0))

    def whole(shape):
        return pl.BlockSpec(shape, lambda i: (0,) * len(shape))

    keys_updated, values_updated, log_normalizer, picked = pl.pallas_call(
        emit_kernel,
        name="emit",
        grid=(slots // block,),
        out_shape=(
            jax.ShapeDtypeStruct((slots, 256), BF16),
            jax.ShapeDtypeStruct((slots, 256), BF16),
            jax.ShapeDtypeStruct((5, 4, 48), F32),
            jax.ShapeDtypeStruct((5, 4, 8, 48), F32),
        ),
        in_specs=[
            SM, SM, whole((48, 256)), whole((48, 256)), whole((2, 8, 640)), rowspec, rowspec,
        ],
        out_specs=(rowspec, rowspec, whole((5, 4, 48)), whole((5, 4, 8, 48))),
        compiler_params=pltpu.CompilerParams(vmem_limit_bytes=62 << 20),
    )(cache_length, accepted_path, new_keys, new_values, result, keys, values)
    return (
        keys_updated.reshape(cache_keys.shape),
        values_updated.reshape(cache_values.shape),
        jnp.transpose(log_normalizer, (0, 2, 1)),
        jnp.transpose(picked, (0, 3, 1, 2)),
    )


def solution(mesh):
    placed = (
        P("kv", "vocab", "seq"),
        P("seq", "kv", None),
        P("kv", None, "seq"),
        P("seq"),
        P("seq"),
        P("seq"),
        P("seq"),
        P("seq"),
        P("vocab", "seq", "kv", None),
        P("vocab", "seq", "kv", None),
        P("vocab"),
        P("vocab", None, None),
        P("vocab", None),
        P("seq", None, ("kv", "vocab")),
        P(("kv", "vocab"), "seq"),
        P(None, "seq", ("kv", "vocab")),
        P(None, ("kv", "vocab")),
        P(("kv", "seq", "vocab"), None),
        P(),
    )
    return jax.shard_map(
        local,
        mesh=mesh,
        in_specs=placed,
        out_specs=(P("vocab", "seq", "kv", None), P("vocab", "seq", "kv", None), P(), P()),
        check_vma=False,
    )
```

```python
import jax
import jax.numpy as jnp
import numpy as np
from jax import lax
from jax.experimental import pallas as pl
from jax.experimental.pallas import tpu as pltpu
from jax.sharding import PartitionSpec as P

MESH = pl.DeviceIdType.MESH
F32 = jnp.float32
BF16 = jnp.bfloat16
WIDTH = 3584
EPSILON = 1e-06
SCORE_CAP = 50.0
LOGIT_CAP = 30.0
NT = (((1,), (1,)), ((), ()))


def rem(a, n):
    return lax.rem(a, jnp.int32(n))


def div(a, n):
    return lax.div(a, jnp.int32(n))


def dot(a, b):
    return jnp.dot(a, b, preferred_element_type=F32)


def dot_nt(a, b):
    return lax.dot_general(a, b, NT, preferred_element_type=F32)


def iota(shape, dim):
    return lax.broadcasted_iota(jnp.int32, shape, dim)


def send(src, dst, ssem, rsem, peer):
    pltpu.make_async_remote_copy(
        src_ref=src,
        dst_ref=dst,
        send_sem=ssem,
        recv_sem=rsem,
        device_id=peer,
        device_id_type=MESH,
    ).start()


def wait_bytes(ref, sem):
    pltpu.make_async_copy(ref, ref, sem).wait()


def plane_peer(p, d):
    q = rem(p + d, 32)
    return q, {"kv": div(q, 4), "vocab": rem(q, 4)}


def position_in_mesh():
    return lax.axis_index("kv"), lax.axis_index("seq"), lax.axis_index("vocab")


def capped_weight(scores):
    return jnp.exp(SCORE_CAP * jnp.tanh(scores * (0.0625 / SCORE_CAP)))


def moments(values):
    lane = iota((8, 128), 1)
    tile = jnp.zeros((8, 128), F32)
    for i, v in enumerate(values):
        tile = jnp.where(lane == i, jnp.sum(v, axis=1, keepdims=True), tile)
    return tile


def rms_inverse(total):
    return lax.rsqrt(jnp.maximum(total, 0.0) / WIDTH + EPSILON)


LOADS = (
    "h", "p48", "g_att", "w_in", "freq", "anc", "keys", "values", "e64", "w_out", "g_post",
    "g_pre", "p192", "w_gu", "e256", "w_down", "g_fpost", "g_fin", "w_draft", "bias", "cand",
    "w_voc",
)


def step_kernel(len_ref, *refs):
    count = len(LOADS)
    source = dict(zip(LOADS, refs[:count]))
    kn, vn, res_ref = refs[count : count + 3]
    here = dict(zip(LOADS, refs[count + 3 : 2 * count + 3]))
    (
        wp, spread, pad8, xg, xf6, ps, prc, agc, qs,
        den, num, ns, nr, ga, af, os_, orr, ms, mr, fp, xf, gs, gr, ags, acts, ds, dsr,
        ms2, mr2, npl, nsc, nbz, lf, dsl, dslr, biasf, zbo, zb, bf, big, bbase,
        base4, tokb, tokd, rz, rx, ry, accb, accd,
        wgu, fin, pad6, wsem, ssem, rsem, zr, sring, r1, r2, r2h,
    ) = refs[2 * count + 3 :]
    kv, z, y = position_in_mesh()
    core = rem(kv, 2)
    x = div(kv, 2)
    p = kv * 4 + y
    sibling = kv + 1 - 2 * core
    barrier = pltpu.get_barrier_semaphore()

    @pl.loop(1, 32)
    def _(d):
        pl.semaphore_signal(barrier, inc=1, device_id=plane_peer(p, d)[1], device_id_type=MESH)

    for d in (4, 3, 5, 2, 6, 1, 7):
        other = rem(z + d, 8)
        pl.semaphore_signal(barrier, inc=1, device_id={"seq": other}, device_id_type=MESH)
        pl.semaphore_signal(barrier, inc=1, device_id={"kv": sibling, "seq": other}, device_id_type=MESH)
    copies = {}
    for i, name in enumerate(LOADS):
        copies[name] = pltpu.make_async_copy(source[name], here[name], wsem.at[i])
        copies[name].start()

    def get(name):
        copies[name].wait()
        return here[name]

    sent = []

    def to_seq(src, dst, s, total):
        for d in (4, 3, 5, 2, 6, 1, 7):
            other = rem(z + d, 8)
            send(src(other), dst(d), ssem.at[s], rsem.at[s], {"seq": other})
        sent.append((total, s))

    def to_kv(src, dst, s, total):
        for d in (4, 5, 3, 2, 6, 1, 7):
            other = rem(kv + d, 8)
            send(src(other), dst(d), ssem.at[s], rsem.at[s], {"kv": other})
        sent.append((total, s))

    def to_plane(src, dst, s, total):
        @pl.loop(0, 31)
        def _(i):
            d = rem(i + 14, 31) + 1
            q, peer = plane_peer(p, d)
            send(src(q), dst(d), ssem.at[s], rsem.at[s], peer)

        sent.append((total, s))

    pad8[...] = jnp.zeros_like(pad8)
    pad6[...] = jnp.zeros_like(pad6)
    xf[...] = jnp.zeros_like(xf)
    pad8[0:6, :] = get("h")[...].astype(F32)
    xg[kv] = pad8[...].astype(BF16)
    pl.semaphore_wait(barrier, 45)
    to_kv(lambda o: xg.at[kv], lambda d: xg.at[kv], 0, xg.at[0:7])
    depth = jnp.sum(get("anc")[...].astype(F32), axis=1, keepdims=True) - 1.0
    angle = (len_ref[0].astype(F32) + depth) * get("freq")[...]
    cosine = jnp.cos(angle)
    sine = jnp.sin(angle)
    eye = iota((96, 128), 0) == iota((96, 128), 1)
    p48 = get("p48")
    gain = get("g_att")[...]
    w_in = get("w_in")
    wait_bytes(xg.at[0:7], rsem.at[0])
    for j in range(8):
        xf6[8 * j : 8 * j + 8, :] = xg[j].astype(F32)
    tokens = dot(p48[...], xf6[...].astype(BF16))
    squares = jnp.sum(tokens * tokens, axis=1, keepdims=True)
    row = jnp.sum(jnp.where(eye[0:48], squares, 0.0), axis=0, keepdims=True)
    row = jnp.broadcast_to(row, (8, 128)).astype(BF16)
    part = dot((tokens * gain).astype(BF16), w_in[...])
    for j in range(8):
        ps[j, 0:48, :] = part[:, 128 * j : 128 * j + 128].astype(BF16)
        ps[j, 48:56, :] = row
    to_seq(lambda o: ps.at[o], lambda d: prc.at[d - 1], 1, prc)
    lane = iota((896, 1024), 1)
    inside = lane & 127
    place = lax.shift_right_logical(lane, 7) * 112 + inside
    spread[...] = jnp.where((iota((896, 1024), 0) == place) & (inside < 112), 1.0, 0.0).astype(BF16)
    wait_bytes(prc, rsem.at[1])
    chunk = ps[z].astype(F32)
    for j in range(7):
        chunk = chunk + prc[j].astype(F32)
    column = jnp.sum(jnp.where(eye[0:48], chunk[48:49, :], 0.0), axis=1, keepdims=True)
    agc[z] = (chunk[0:48] * rms_inverse(column)).astype(BF16)
    to_seq(lambda o: agc.at[z], lambda d: agc.at[z], 2, agc.at[0:7])
    keys, values = get("keys"), get("values")
    wait_bytes(agc.at[0:7], rsem.at[2])
    for j, (ref, row0) in enumerate(((qs, 0), (qs, 48), (kn, 0))):
        first = agc[2 * j].astype(F32)
        second = agc[2 * j + 1].astype(F32)
        ref[row0 : row0 + 48, 0:128] = (first * cosine - second * sine).astype(BF16)
        ref[row0 : row0 + 48, 128:256] = (second * cosine + first * sine).astype(BF16)
    vn[:, 0:128] = agc[6]
    vn[:, 128:256] = agc[7]

    queries = qs[...]
    anc = jnp.where(z == 0, here["anc"][...], 0)
    anc = jnp.concatenate([anc, anc], axis=0)
    weights = capped_weight(dot_nt(queries, kn[...]))
    weights = jnp.where(anc > 0, weights, 0.0)
    den[...] = jnp.sum(weights, axis=1, keepdims=True)
    num[...] = dot(weights.astype(BF16), vn[...])
    filled = len_ref[0] - z * 2048

    @pl.loop(0, 4)
    def _(i):
        rows = pl.ds(pl.multiple_of(i * 512, 512), 512)
        weights = capped_weight(dot_nt(queries, keys[rows, :]))
        weights = jnp.where(iota((96, 512), 1) < filled - i * 512, weights, 0.0)
        den[...] += jnp.sum(weights, axis=1, keepdims=True)
        num[...] += dot(weights.astype(BF16), values[rows, :])

    row = jnp.sum(jnp.where(eye, den[...], 0.0), axis=0, keepdims=True)
    row = jnp.broadcast_to(row, (16, 128)).astype(BF16)
    for j in range(8):
        r0, c0 = 24 * (j // 2), 128 * (j % 2)
        ns[j, 0:16, :] = row
        ns[j, 16:40, :] = num[r0 : r0 + 24, c0 : c0 + 128].astype(BF16)
    to_seq(lambda o: ns.at[o], lambda d: nr.at[d - 1], 3, nr)
    raw_gu = get("w_gu")

    def relay_out(i):
        rows = slice(112 * i, 112 * i + 112)
        wgu[rows, 0:448] = raw_gu[rows, 0, :]
        wgu[rows, 448:896] = raw_gu[rows, 1, :]

    relay_out(0)
    relay_out(1)
    e64, w_out = get("e64"), get("w_out")
    wait_bytes(nr, rsem.at[3])
    total = ns[z].astype(F32)
    for j in range(7):
        total = total + nr[j].astype(F32)
    chosen = iota((24, 128), 1) == iota((24, 128), 0) + 24 * div(z, 2)
    below = jnp.sum(jnp.where(chosen, total[0:1, :], 0.0), axis=1, keepdims=True)
    ga[z] = (total[16:40, :] / below).astype(BF16)
    to_seq(lambda o: ga.at[z], lambda d: ga.at[z], 4, ga.at[0:7])
    relay_out(2)
    relay_out(3)
    w_voc = get("w_voc")

    def widen(j):
        wp[0:512, 1024 * j : 1024 * j + 1024] = dot(
            w_voc[:, 896 * j : 896 * j + 896], spread[...]
        ).astype(BF16)

    wait_bytes(ga.at[0:7], rsem.at[4])
    for j in range(8):
        r0, c0 = 24 * ((j // 2) % 2), 256 * (j // 4) + 128 * (j % 2)
        af[r0 : r0 + 24, c0 : c0 + 128] = ga[j].astype(F32)
    attended = dot(e64[...], af[...].astype(BF16)).astype(BF16)
    out = dot_nt(attended, w_out[...])
    for j in range(8):
        os_[j] = out[8 * j : 8 * j + 8, :].astype(BF16)
    to_kv(lambda o: os_.at[o], lambda d: orr.at[d - 1], 5, orr)
    hidden = pad8[...]
    gain = get("g_post")[...]
    wait_bytes(orr, rsem.at[5])
    att = os_[kv].astype(F32)
    for j in range(7):
        att = att + orr[j].astype(F32)
    gained = att * gain
    ms[...] = moments((att * att, hidden * gained, gained * gained, hidden * hidden))
    to_seq(lambda o: ms, lambda d: mr.at[d - 1], 6, mr)
    gain = get("g_pre")[...]
    wait_bytes(mr, rsem.at[6])
    tot = ms[...]
    for j in range(7):
        tot = tot + mr[j]
    inv = rms_inverse(tot[:, 0:1])
    first = (hidden + gained * inv).astype(BF16).astype(F32)
    inv = rms_inverse(tot[:, 3:4] + 2.0 * inv * tot[:, 1:2] + inv * inv * tot[:, 2:3])
    fp[p] = (first * inv * gain)[0:6].astype(BF16)
    to_plane(lambda q: fp.at[p], lambda d: fp.at[p], 7, fp.at[0:31])
    widen(0)
    p192 = get("p192")
    wait_bytes(fp.at[0:31], rsem.at[7])
    for j in range(32):
        xf[8 * j : 8 * j + 6, :] = fp[j].astype(F32)
    rows192 = dot(p192[...], xf[...].astype(BF16)).astype(BF16)
    gu = dot(rows192, wgu[...])
    for j in range(8):
        gs[j] = gu[24 * j : 24 * j + 24, :].astype(BF16)
    to_seq(lambda o: gs.at[o], lambda d: gr.at[d - 1], 8, gr)
    widen(1)
    widen(2)
    widen(3)
    send(wp.at[0:512], wp.at[512:1024], ssem.at[17], rsem.at[17], {"kv": sibling})
    sent.append((wp.at[0:512], 17))
    e256, w_down = get("e256"), get("w_down")
    wait_bytes(gr, rsem.at[8])
    gu = gs[z].astype(F32)
    for j in range(7):
        gu = gu + gr[j].astype(F32)
    gate, up = gu[:, 0:448], gu[:, 448:896]
    gelu = 0.5 * gate * (1.0 + jnp.tanh(0.7978845608028654 * (gate + 0.044715 * gate * gate * gate)))
    ags[z] = (gelu * up).astype(BF16)
    to_seq(lambda o: ags.at[z], lambda d: ags.at[z], 9, ags.at[0:7])
    cand = get("cand")
    for n in range(5):
        for k in range(2):
            ids = cand[n, 2 * core + k]
            if n == 0:
                tokb[:, 48 * k : 48 * k + 48] = ids
            else:
                at = 96 * (n - 1) + 48 * k
                tokd[:, at : at + 48] = ids
    lf[...] = jnp.zeros_like(lf)
    biasf[...] = jnp.zeros_like(biasf)
    biasf[0:4, 0:112] = get("bias")[...]
    accb[...] = jnp.zeros_like(accb)
    base4[...] = jnp.zeros_like(base4)
    accd[...] = jnp.zeros_like(accd)
    wait_bytes(ags.at[0:7], rsem.at[9])
    for j in range(8):
        acts[24 * j : 24 * j + 24, :] = ags[j].astype(F32)
    act = dot(e256[...], acts[...].astype(BF16)).astype(BF16)
    out = dot(act, w_down[...])
    for j in range(32):
        ds[j] = out[8 * j : 8 * j + 6, :].astype(BF16)
    to_plane(lambda q: ds.at[q], lambda d: dsr.at[d - 1], 10, dsr)
    gain = get("g_fpost")[...]
    wait_bytes(dsr, rsem.at[10])
    out = ds[p].astype(F32)
    for j in range(31):
        out = out + dsr[j].astype(F32)
    pad6[0:6, :] = out
    out = pad6[...]
    gained = out * gain
    ms2[...] = moments((out * out, first * gained, gained * gained, first * first))
    to_seq(lambda o: ms2, lambda d: mr2.at[d - 1], 11, mr2)
    gain = get("g_fin")[...]
    w_draft = get("w_draft")
    wait_bytes(mr2, rsem.at[11])
    tot = ms2[...]
    for j in range(7):
        tot = tot + mr2[j]
    inv = rms_inverse(tot[:, 0:1])
    second = (first + gained * inv).astype(BF16).astype(F32)
    inv = rms_inverse(tot[:, 3:4] + 2.0 * inv * tot[:, 1:2] + inv * inv * tot[:, 2:3])
    normed = second * inv * gain
    npl[p] = normed[0:6].astype(BF16)
    to_plane(lambda q: npl.at[p], lambda d: npl.at[p], 12, npl.at[0:31])
    wait_bytes(npl.at[0:31], rsem.at[12])
    for j in range(32):
        xf[8 * j : 8 * j + 6, :] = npl[j].astype(F32)
    rows192 = dot(p192[...], xf[...].astype(BF16)).astype(BF16)
    halves = (slice(0, 2), slice(2, 4))
    for h, (lifted_sem, pair) in enumerate(((13, halves[0]), (14, halves[1]))):
        for i in (2 * h, 2 * h + 1):
            lf[i, :, 0:112] = dot(rows192, w_draft[i])
            for j in range(8):
                dsl[j, i] = lf[i, 24 * j : 24 * j + 24, :].astype(BF16)
        to_seq(
            lambda o: dsl.at[o, pair], lambda d: dslr.at[d - 1, pair], lifted_sem, dslr.at[:, pair]
        )
    nsc[0] = rows192[0:96]
    nsc[1] = rows192[96:192]
    reader = 2 * x + div(z, 4)
    keep = core == div(z, 4)
    for h, (lifted_sem, group_sem, pair) in enumerate(((13, 16, halves[0]), (14, 20, halves[1]))):
        wait_bytes(dslr.at[:, pair], rsem.at[lifted_sem])
        for i in (2 * h, 2 * h + 1):
            lifted = dsl[z, i].astype(F32)
            for j in range(7):
                lifted = lifted + dslr[j, i].astype(F32)
            lifted = lifted + biasf[i : i + 1, :]
            zbo[i] = (lifted / (1.0 + jnp.exp(-lifted))).astype(BF16)
        mine, landing = zbo.at[pair], zb.at[core, rem(z, 4), pair]
        for d in (4, 3, 5, 2, 6, 1, 7):
            send(mine, landing, ssem.at[group_sem], rsem.at[group_sem], {"kv": reader, "seq": rem(z + d, 8)})

        @pl.when(jnp.logical_not(keep))
        def _():
            send(mine, landing, ssem.at[group_sem], rsem.at[group_sem], {"kv": sibling})

        @pl.when(keep)
        def _():
            pltpu.make_async_copy(mine, landing, rsem.at[group_sem]).start()

        sent.append((zb.at[0, 0:4, pair], group_sem))
        sent.append((zb.at[0, 0:3, pair], group_sem))
    nbz[z] = nsc[core]

    def along_seq(ref, step, sem):
        send(ref, ref, ssem.at[15], sem, {"seq": rem(z + step + 8, 8)})

    sent.append((nbz.at[0:7], 15))
    along_seq(nbz.at[z], 1, zr.at[0, 0])
    along_seq(nbz.at[z], -1, zr.at[0, 1])

    def base_on(k):
        wait_bytes(nbz.at[0], zr.at[k - 1, 0])
        left = nbz.at[rem(z - k + 8, 8)]
        along_seq(left if k < 3 else left.at[0:48], 1, zr.at[k, 0])
        wait_bytes(nbz.at[0], zr.at[k - 1, 1])
        right = nbz.at[rem(z + k, 8)]
        along_seq(right if k < 3 else right.at[48:96], -1, zr.at[k, 1])

    def block(h, s, o, t, part=None):
        bx, by = (x + o, y + t) if s == 0 else (x + t, y + o)
        at = pl.multiple_of(((2 * rem(bx + 4, 4) + s) * 4 + rem(by + 4, 4)) * 128, 128)
        if part is None:
            return big.at[2 * h : 2 * h + 2, :, pl.ds(at, 128)]
        return big.at[2 * h + part : 2 * h + part + 1, :, pl.ds(at, 128)]

    def neighbour(axis, step):
        if axis == 0:
            return {"kv": rem(kv + 2 * step + 8, 8)}
        return {"vocab": rem(y + step + 4, 4)}

    def ring(ref, s, axis, step, sem):
        send(ref, ref, sring.at[s], sem, neighbour(axis, step))

    offsets = (0, -1, 1, 2)

    def second_axis(h, s, oi):
        ref = block(h, s, offsets[oi], 0)
        ring(ref, s, 1 - s, 1, r2.at[h, s, oi, 0])
        ring(ref, s, 1 - s, -1, r2.at[h, s, oi, 1])

    def pass_on(h, s, oi):
        wait_bytes(block(h, s, 0, 0), r2.at[h, s, oi, 0])
        ring(block(h, s, offsets[oi], -1, 0), s, 1 - s, 1, r2h.at[h, s, oi, 0])
        wait_bytes(block(h, s, 0, 0), r2.at[h, s, oi, 1])
        ring(block(h, s, offsets[oi], 1, 1), s, 1 - s, -1, r2h.at[h, s, oi, 1])

    both = tuple((h, s) for h in range(2) for s in range(2))
    for h, (group_sem, pair) in enumerate(((16, halves[0]), (20, halves[1]))):
        wait_bytes(zb.at[:, :, pair], rsem.at[group_sem])
        for s in range(2):
            own = block(h, s, 0, 0)
            for i in range(2):
                for j in range(4):
                    bf[i, 24 * j : 24 * j + 24, :] = zb[s, j, 2 * h + i].astype(F32)
                own[i] = bf[i].astype(BF16)
            ring(own, s, s, 1, r1.at[h, s, 0])
            ring(own, s, s, -1, r1.at[h, s, 1])
            second_axis(h, s, 0)

    mine = ((kv * 8 + z) * 4 + y) * 512
    theirs = ((sibling * 8 + z) * 4 + y) * 512

    def score(raw, ids, acc, lanes, i):
        logits = LOGIT_CAP * jnp.tanh(raw * (1.0 / LOGIT_CAP))
        entry = iota(raw.shape, 0)
        wanted = ids - (mine + 256 * i if i < 2 else theirs + 256 * (i - 2))
        for c in range(8):
            hit = entry == wanted[c : c + 1, :]
            acc[c : c + 1, 0:lanes] += jnp.sum(jnp.where(hit, logits, 0.0), axis=0, keepdims=True)
        acc[8:9, 0:lanes] += jnp.sum(jnp.exp(logits), axis=0, keepdims=True)

    def base(i):
        raw = dot_nt(wp[256 * i : 256 * i + 256, :], bbase[...])
        for d in range(4):
            base4[256 * i : 256 * i + 256, 96 * d : 96 * d + 96] += raw
        score(raw, tokb[:, 0:96], accb, 96, i)

    def add_columns(s, bx):
        at = pl.ds(pl.multiple_of((2 * rem(bx + 4, 4) + s) * 512, 512), 512)
        fresh = big[:, :, at].reshape(384, 512)
        for i in range(4):
            rows = slice(256 * i, 256 * i + 256)
            base4[rows, :] += dot_nt(wp[rows, at], fresh)

    def last_halves(s, oi):
        for h in range(2):
            wait_bytes(block(h, s, 0, 0, 0), r2h.at[h, s, oi, 0])
            wait_bytes(block(h, s, 0, 0, 1), r2h.at[h, s, oi, 1])

    for h, s in both:
        wait_bytes(block(h, s, 0, 0), r1.at[h, s, 0])
        ring(block(h, s, -1, 0, 0), s, s, 1, r1.at[h, s, 2])
        second_axis(h, s, 1)
        wait_bytes(block(h, s, 0, 0), r1.at[h, s, 1])
        ring(block(h, s, 1, 0, 1), s, s, -1, r1.at[h, s, 3])
        second_axis(h, s, 2)
    wait_bytes(wp.at[0:512], rsem.at[17])
    base_on(1)
    for h, s in both:
        pass_on(h, s, 0)
    for h, s in both:
        wait_bytes(block(h, s, 0, 0, 0), r1.at[h, s, 2])
        wait_bytes(block(h, s, 0, 0, 1), r1.at[h, s, 3])
        second_axis(h, s, 3)
    base_on(2)
    for h, s in both:
        pass_on(h, s, 1)
    add_columns(1, x)
    base_on(3)
    for h, s in both:
        pass_on(h, s, 2)
    last_halves(0, 0)
    add_columns(0, x)
    for h, s in both:
        pass_on(h, s, 3)
    wait_bytes(nbz.at[0, 0:48], zr.at[3, 0])
    wait_bytes(nbz.at[0, 0:48], zr.at[3, 1])
    for j in range(8):
        bbase[:, 512 * j : 512 * j + 512] = dot(nbz[j], spread[0:448, 0:512]).astype(BF16)
    for i in range(4):
        base(i)
    last_halves(0, 1)
    add_columns(0, x - 1)
    add_columns(1, x - 1)
    add_columns(1, x + 1)
    last_halves(0, 2)
    add_columns(0, x + 1)
    last_halves(0, 3)
    add_columns(0, x + 2)
    for oi in range(4):
        last_halves(1, oi)
    add_columns(1, x + 2)
    for i in range(4):
        score(base4[256 * i : 256 * i + 256, :], tokd[...], accd, 384, i)

    fin[...] = jnp.zeros_like(fin)
    fin[:, 0:96] = accb[0:8, 0:96]
    fin[:, 128:512] = accd[0:8, :]
    fin[0:1, 512:608] = accb[8:9, 0:96]
    for d in range(4):
        fin[d + 1 : d + 2, 512:608] = accd[8:9, 96 * d : 96 * d + 96]
    rz[z] = fin[...].astype(BF16)
    to_seq(lambda o: rz.at[z], lambda d: rz.at[z], 18, rz.at[0:7])
    wait_bytes(rz.at[0:7], rsem.at[18])

    def add_up(slots, count):
        res = slots[0].astype(F32)
        for j in range(1, count):
            res = res + slots[j].astype(F32)
        return res

    rx[x] = add_up(rz, 8).astype(BF16)
    for d in (2, 1, 3):
        send(rx.at[x], rx.at[x], ssem.at[19], rsem.at[19], {"kv": rem(kv + 2 * d, 8)})
    wait_bytes(rx.at[0:3], rsem.at[19])
    ry[core * 4 + y] = add_up(rx, 4).astype(BF16)
    place = ry.at[core * 4 + y]
    for d in (2, 1, 3, 0):
        other = rem(y + d, 4)
        send(place, place, ssem.at[21], rsem.at[21], {"kv": sibling, "vocab": other})
        if d:
            send(place, place, ssem.at[21], rsem.at[21], {"vocab": other})
    sent.append((rx.at[0:3], 19))
    sent.append((ry.at[0:7], 21))
    wait_bytes(ry.at[0:7], rsem.at[21])
    for c in range(2):
        res_ref[c] = add_up(ry.at[4 * c : 4 * c + 4], 4)

    for ref, s in sent:
        wait_bytes(ref, ssem.at[s])

    @pl.when(jnp.logical_not(keep))
    def _():
        wait_bytes(zbo.at[halves[0]], ssem.at[16])
        wait_bytes(zbo.at[halves[1]], ssem.at[20])

    for s in range(2):
        wait_bytes(big.at[:, :, 0:1920], sring.at[s])


def emit_kernel(
    len_ref, path_ref, kn_ref, vn_ref, res_ref, keys_ref, values_ref,
    keys_out, values_out, logn_ref, pick_ref,
):
    step = pl.program_id(0)
    rows = keys_ref.shape[0]
    length = len_ref[0]
    start = lax.axis_index("seq") * (rows * pl.num_programs(0)) + step * rows
    keys = keys_ref[...]
    values = values_ref[...]
    keys_out[...] = keys
    values_out[...] = values

    @pl.when((start + rows > length) & (start < length + 5))
    def _():
        away = start + iota((rows, 1), 0) - length
        target = jnp.full((rows, 1), -1, jnp.int32)
        for a in range(5):
            target = jnp.where(away == a, path_ref[0, a], target)
        selector = jnp.where(iota((rows, 48), 1) == target, 1.0, 0.0).astype(BF16)
        inside = jnp.broadcast_to(target, (rows, 256)) >= 0
        for fresh, old, out in ((kn_ref, keys, keys_out), (vn_ref, values, values_out)):
            out[...] = jnp.where(inside, dot(selector, fresh[...]), old.astype(F32)).astype(BF16)

    @pl.when(step == 0)
    def _():
        for c in range(2):
            for n in range(5):
                logs = jnp.log(res_ref[c, n : n + 1, 512:608])
                for k in range(2):
                    lane = 48 * k if n == 0 else 128 + 96 * (n - 1) + 48 * k
                    logn_ref[n, 2 * c + k : 2 * c + k + 1, :] = logs[:, 48 * k : 48 * k + 48]
                    pick_ref[n, 2 * c + k] = res_ref[c, 0:8, lane : lane + 48]


def one_hot_rows(rows, columns, places):
    table = np.zeros((rows, columns), np.float32)
    table[np.arange(rows), places] = 1.0
    return table


def tables():
    r48 = np.arange(48)
    p48 = one_hot_rows(48, 64, (r48 // 6) * 8 + r48 % 6)
    r192 = np.arange(192)
    tenant, node = r192 // 48, r192 % 48
    p192 = one_hot_rows(192, 256, ((node // 6) * 4 + tenant) * 8 + node % 6)
    return p48, p192


def vmem(shape, dtype=BF16):
    return pltpu.VMEM(shape, dtype)


VM = pl.BlockSpec(memory_space=pltpu.VMEM)
SM = pl.BlockSpec(memory_space=pltpu.SMEM)
ANY = pl.BlockSpec(memory_space=pl.ANY)
DMA = pltpu.SemaphoreType.DMA


HBM = pl.BlockSpec(memory_space=pltpu.HBM)


def local(
    hidden_state,
    input_projection,
    output_projection,
    norm_pre_attention,
    norm_post_attention,
    norm_pre_feedforward,
    norm_post_feedforward,
    norm_final,
    cache_keys,
    cache_values,
    cache_length,
    ancestors,
    accepted_path,
    gate_up_weight,
    down_weight,
    draft_weight,
    draft_bias,
    vocab_weight,
    candidate_tokens,
):
    p48, p192 = (jnp.asarray(t, BF16) for t in tables())
    frequency = jnp.asarray(
        (10000.0 ** (-2.0 * np.arange(128, dtype=np.float64) / 256)).astype(np.float32)
    )
    slots = cache_keys.shape[1]
    keys = cache_keys.reshape(slots, 256)
    values = cache_values.reshape(slots, 256)
    arrays = dict(
        h=hidden_state.reshape(6, 448),
        p48=p48,
        g_att=norm_pre_attention.reshape(1, 448),
        w_in=input_projection.reshape(448, 1024),
        freq=frequency.reshape(1, 128),
        anc=ancestors[0],
        keys=keys,
        values=values,
        e64=p48.T,
        w_out=output_projection[0].T,
        g_post=norm_post_attention.reshape(1, 448),
        g_pre=norm_pre_feedforward.reshape(1, 448),
        p192=p192,
        w_gu=gate_up_weight,
        e256=p192.T,
        w_down=down_weight,
        g_fpost=norm_post_feedforward.reshape(1, 448),
        g_fin=norm_final.reshape(1, 448),
        w_draft=draft_weight,
        bias=draft_bias,
        cand=jnp.transpose(candidate_tokens, (0, 2, 3, 1)),
        w_voc=vocab_weight,
    )
    operands = [arrays[name] for name in LOADS]
    new_keys, new_values, result = pl.pallas_call(
        step_kernel,
        name="step",
        out_shape=(
            jax.ShapeDtypeStruct((48, 256), BF16),
            jax.ShapeDtypeStruct((48, 256), BF16),
            jax.ShapeDtypeStruct((2, 8, 640), F32),
        ),
        in_specs=[SM] + [HBM] * len(LOADS),
        out_specs=(VM, VM, VM),
        scratch_shapes=[vmem(a.shape, a.dtype) for a in operands] + [
            vmem((1024, 4096)), vmem((896, 1024)), vmem((8, 448), F32), vmem((8, 8, 448)),
            vmem((64, 448), F32), vmem((8, 56, 128)), vmem((7, 56, 128)), vmem((8, 48, 128)),
            vmem((96, 256)),
            vmem((96, 1), F32), vmem((96, 256), F32), vmem((8, 40, 128)), vmem((7, 40, 128)),
            vmem((8, 24, 128)), vmem((48, 512), F32), vmem((8, 8, 448)), vmem((7, 8, 448)),
            vmem((8, 128), F32), vmem((7, 8, 128), F32), vmem((32, 6, 448)), vmem((256, 448), F32),
            vmem((8, 24, 896)), vmem((7, 24, 896)), vmem((8, 24, 448)), vmem((192, 448), F32),
            vmem((32, 6, 448)), vmem((31, 6, 448)),
            vmem((8, 128), F32), vmem((7, 8, 128), F32), vmem((32, 6, 448)),
            vmem((2, 96, 448)), vmem((8, 96, 448)),
            vmem((4, 192, 128), F32), vmem((8, 4, 24, 128)), vmem((7, 4, 24, 128)),
            vmem((8, 128), F32), vmem((4, 24, 128)), vmem((2, 4, 4, 24, 128)),
            vmem((2, 96, 128), F32), vmem((4, 96, 4096)), vmem((96, 4096)),
            vmem((1024, 384), F32), vmem((8, 128), jnp.int32), vmem((8, 384), jnp.int32),
            vmem((8, 8, 640)), vmem((4, 8, 640)), vmem((8, 8, 640)),
            vmem((16, 128), F32), vmem((16, 384), F32),
            vmem((448, 896)), vmem((8, 640), F32), vmem((8, 448), F32),
            DMA((len(LOADS),)), DMA((23,)), DMA((23,)), DMA((4, 2)), DMA((2,)), DMA((2, 2, 4)), DMA((2, 2, 4, 2)),
            DMA((2, 2, 4, 2)),
        ],
        compiler_params=pltpu.CompilerParams(
            collective_id=0, has_side_effects=True, vmem_limit_bytes=62 << 20
        ),
    )(cache_length, *operands)
    block = 1024
    rowspec = pl.BlockSpec((block, 256), lambda i: (i, 0))

    def whole(shape):
        return pl.BlockSpec(shape, lambda i: (0,) * len(shape))

    keys_updated, values_updated, log_normalizer, picked = pl.pallas_call(
        emit_kernel,
        name="emit",
        grid=(slots // block,),
        out_shape=(
            jax.ShapeDtypeStruct((slots, 256), BF16),
            jax.ShapeDtypeStruct((slots, 256), BF16),
            jax.ShapeDtypeStruct((5, 4, 48), F32),
            jax.ShapeDtypeStruct((5, 4, 8, 48), F32),
        ),
        in_specs=[
            SM, SM, whole((48, 256)), whole((48, 256)), whole((2, 8, 640)), rowspec, rowspec,
        ],
        out_specs=(rowspec, rowspec, whole((5, 4, 48)), whole((5, 4, 8, 48))),
        compiler_params=pltpu.CompilerParams(vmem_limit_bytes=62 << 20),
    )(cache_length, accepted_path, new_keys, new_values, result, keys, values)
    return (
        keys_updated.reshape(cache_keys.shape),
        values_updated.reshape(cache_values.shape),
        jnp.transpose(log_normalizer, (0, 2, 1)),
        jnp.transpose(picked, (0, 3, 1, 2)),
    )


def solution(mesh):
    placed = (
        P("kv", "vocab", "seq"),
        P("seq", "kv", None),
        P("kv", None, "seq"),
        P("seq"),
        P("seq"),
        P("seq"),
        P("seq"),
        P("seq"),
        P("vocab", "seq", "kv", None),
        P("vocab", "seq", "kv", None),
        P("vocab"),
        P("vocab", None, None),
        P("vocab", None),
        P("seq", None, ("kv", "vocab")),
        P(("kv", "vocab"), "seq"),
        P(None, "seq", ("kv", "vocab")),
        P(None, ("kv", "vocab")),
        P(("kv", "seq", "vocab"), None),
        P(),
    )
    return jax.shard_map(
        local,
        mesh=mesh,
        in_specs=placed,
        out_specs=(P("vocab", "seq", "kv", None), P("vocab", "seq", "kv", None), P(), P()),
        check_vma=False,
    )
```
